128 devices in a mesh: rows: 16 (over y, x), cols: 8 (over z, core).
Axes of the slice: x: 4, y: 4, z: 4, core: 2. Of those that a mesh axis runs over, the one named last changes fastest.
Arguments:
- ensemble: bfloat16 [64, 768, 1024], P(None, 'rows', 'cols'), may hold values from -6 to 6
- row_profile: bfloat16 [768, 16384], P('rows'), may hold values from 0.0072021484 to 0.071777344
- col_profile: bfloat16 [1024, 16384], P('cols'), may hold values from 0.006225586 to 0.0625
- obs_owned: float32 [128, 384], P(('rows', 'cols')), may hold values from -18 to 18
- noise_owned: float32 [128, 384], P(('rows', 'cols')), may hold values from 40.96 to 409.6
- block_owner: int32 [128], replicated, may hold values from 0 to 127, as said below
Outputs:
- updated: bfloat16 [64, 768, 1024], P(None, 'rows', 'cols')
The draws below stay inside these ranges and needn't reach their ends.
Inputs may be any that keep to these rules, and one draw needn't show every extreme that they name: `block_owner`: each of the 128 devices owns at most 3 detector blocks, and some devices own exactly 3, some own 1 and some own none.
All inputs are finite; a program needn't handle non-finite values.
Results may differ from the reference program's by a relative error of at most 0.0011.
Values sent between devices are 32-bit elements; how exact they have to be, the bound alone decides.
A program may use at most 128 MiB of HBM per device.

```python
import math
import jax
import jax.numpy as jnp
from jax import lax

MEMBERS = 64
BLOCK = 128
CAP = 3
GRID_ROWS = 768
GRID_COLS = 1024
BLOCKS = 128
DETECTORS = 16384
DEVICES = 128


def draw_block_owner(key, part):
    key_order, key_owner = jax.random.split(jax.random.fold_in(key, 11))
    position = jax.random.permutation(key_order, BLOCKS)
    owner_order = jax.random.permutation(key_owner, DEVICES)
    groups = DEVICES // (2 * CAP)
    heavy_rows = groups * CAP
    slot_index = jnp.where(position < heavy_rows, position // CAP, groups + position - heavy_rows)
    return owner_order[slot_index].astype(jnp.int32)


def levels(stream_key, shape, cuts, least, high):
    def one(dim, parts):
        heights = jax.random.uniform(jax.random.fold_in(jax.random.fold_in(stream_key, 6), dim), (parts,), jnp.float32, least / len(cuts), high / len(cuts))
        return jnp.repeat(jnp.exp(heights), shape[dim] // parts).reshape((-1,) + (1,) * (len(shape) - dim - 1))

    gain = one(*cuts[0])
    for cut in cuts[1:]:
        gain = gain * one(*cut)
    return gain


def scatter_about(key, shape, deviation, limit, pieces=(), kind=jnp.bfloat16):
    drawn = deviation * jax.random.normal(key, shape, jnp.float32)
    if pieces:
        drawn = drawn * levels(key, shape, pieces, -0.22, 0.18)
    return jnp.clip(drawn, -limit, limit).astype(kind)


def setup_inputs(seed: int = 0) -> dict:
    key_list = jax.random.split(jax.random.key(seed), 7)
    return {
        "ensemble": scatter_about(key_list[0], (MEMBERS, GRID_ROWS, GRID_COLS), 1.0, 6.0, ((1, 16), (2, 8))),
        "row_profile": jnp.clip(jnp.exp(math.log(0.071777344) - 2.2991895 * jax.random.uniform(key_list[1], (GRID_ROWS, DETECTORS), jnp.float32) ** levels(key_list[1], (GRID_ROWS, DETECTORS), ((0, 16),), -0.2, 0.2)), 0.0072021484, 0.071777344).astype(jnp.bfloat16),
        "col_profile": jnp.clip(jnp.exp(math.log(0.0625) - 2.306499 * jax.random.uniform(key_list[2], (GRID_COLS, DETECTORS), jnp.float32) ** levels(key_list[2], (GRID_COLS, DETECTORS), ((0, 8),), -0.2, 0.2)), 0.006225586, 0.0625).astype(jnp.bfloat16),
        "obs_owned": scatter_about(key_list[3], (DEVICES, CAP * BLOCK), 3.0, 18.0, ((0, 128),), jnp.float32),
        "noise_owned": jnp.clip(jnp.exp(math.log(409.6) - 2.3025851 * jax.random.uniform(key_list[4], (DEVICES, CAP * BLOCK), jnp.float32) ** levels(key_list[4], (DEVICES, CAP * BLOCK), ((0, 128),), -0.2, 0.2)), 40.96, 409.6),
        "block_owner": draw_block_owner(jax.random.fold_in(key_list[6], 71), 0),
    }


def member_stats(predictions, observed, weights):
    member_mean = lax.optimization_barrier(jnp.mean(predictions, axis=1, keepdims=True))
    anomalies = (predictions - member_mean) / math.sqrt(MEMBERS - 1)
    residuals = observed[:, None, :] - predictions
    scaled = anomalies * weights[:, None, :]
    spread_mat = jnp.einsum('sjd,skd->jk', scaled, anomalies, precision=lax.Precision.HIGHEST)
    innovation = jnp.einsum('sjd,skd->jk', scaled, residuals, precision=lax.Precision.HIGHEST)
    return (spread_mat, innovation)

def apply_gain(ensemble, spread_mat, innovation):
    eye_mat = jnp.eye(MEMBERS, dtype=jnp.float32)
    factor = jnp.linalg.cholesky(eye_mat + spread_mat)
    gain_weights = jax.scipy.linalg.cho_solve((factor, True), innovation)
    flat_field = ensemble.astype(jnp.float32).reshape(MEMBERS, -1)
    member_mean = lax.optimization_barrier(jnp.mean(flat_field, axis=0, keepdims=True))
    anomalies = (flat_field - member_mean) / math.sqrt(MEMBERS - 1)
    moved = flat_field + jnp.dot(gain_weights.T, anomalies, precision=lax.Precision.HIGHEST)
    return moved.reshape(ensemble.shape).astype(jnp.bfloat16)

def reference(ensemble, row_profile, col_profile, obs_owned, noise_owned, block_owner):
    flat_field = ensemble.astype(jnp.float32).reshape(MEMBERS * GRID_ROWS, GRID_COLS)
    col_blocks = col_profile.astype(jnp.float32).reshape(GRID_COLS, BLOCKS, BLOCK).transpose(1, 0, 2)
    row_blocks = row_profile.astype(jnp.float32).reshape(GRID_ROWS, BLOCKS, BLOCK).transpose(1, 0, 2)

    def block_terms(pair_args):
        col_part, row_part = pair_args
        along_cols = jnp.dot(flat_field, col_part, precision=lax.Precision.HIGHEST)
        along_cols = along_cols.reshape(MEMBERS, GRID_ROWS, BLOCK)
        return lax.optimization_barrier(jnp.sum(along_cols * row_part[None], axis=1))
    predictions = lax.map(block_terms, (col_blocks, row_blocks))
    block_index = jnp.arange(BLOCKS, dtype=jnp.int32)
    same_owner = block_owner[None, :] == block_owner[:, None]
    earlier = block_index[None, :] < block_index[:, None]
    slot_rank = lax.optimization_barrier(jnp.sum((same_owner & earlier).astype(jnp.int32), axis=1)).astype(jnp.int32)
    obs_slots = obs_owned.reshape(DEVICES, CAP, BLOCK)
    noise_slots = noise_owned.reshape(DEVICES, CAP, BLOCK)
    observed = obs_slots[block_owner, slot_rank]
    variance = noise_slots[block_owner, slot_rank]
    spread_mat, innovation = member_stats(predictions, observed, 1.0 / variance)
    return apply_gain(ensemble, spread_mat, innovation)
```

```python
import functools
import math

import jax
import jax.numpy as jnp
from jax import lax
from jax.experimental import pallas as pl
from jax.experimental.pallas import tpu as pltpu
from jax.sharding import PartitionSpec as P

MEMBERS = 64
BLOCK = 128
CAP = 3
LROWS = 48
LCOLS = 128
STEPS = 16
WIDE = 512
AHEAD = 3
LAG2 = 3
LAG3 = 6
ROOT = math.sqrt(MEMBERS - 1)
MESH = pl.DeviceIdType.MESH
F32 = jnp.float32
BF16 = jnp.bfloat16


def here():
    r = lax.axis_index("rows")
    c = lax.axis_index("cols")
    return r // 4, r % 4, c // 2, c % 2


def device(y, x, z, k):
    return (y * 4 + x, z * 2 + k)


def partial_kernel(
    e_hbm, col_hbm, row_hbm, obs_ref, noise_ref, owner_ref,
    sums_ref, et_hbm,
    e_v, ef, esend, erecv, lhs, col_v, row_v, csend, crecv, rhs, rowf, pa, pb, pc,
    ra1, ra2, ra3, rb1, rb2, rb3, rc1, rc2, rc3, slots, pack, got_core, got,
    e_sem, et_sem, col_sem, row_sem,
    es_sem, er_sem, cs_sem, cr_sem,
    sa, sb, sc,
    qa1, qa2, qa3, qb1, qb2, qb3, qc1, qc2, qc3,
    so, qo_z, qo_x, qo_y, qo_k,
    st, qt,
):
    y, x, z, k = here()
    sibling = device(y, x, z, 1 - k)

    def zpeer(d):
        return device(y, x, (z + d) % 4, k)

    def xpeer(d):
        return device(y, (x + d) % 4, z, k)

    def ypeer(d):
        return device((y + d) % 4, x, z, k)

    def remote(src, dst, send, recv, to):
        return pltpu.make_async_remote_copy(
            src_ref=src, dst_ref=dst, send_sem=send, recv_sem=recv,
            device_id=to, device_id_type=MESH,
        )

    def sent(src, sem):
        remote(src, src, sem, sem, sibling).wait_send()

    def landed(dst, sem):
        remote(dst, dst, sem, sem, sibling).wait_recv()

    def span(core, s):
        dz, dx = 3 - s // 4, 3 - s % 4
        first = ((core * 4 + (z + dz) % 4) * 4 + (x + dx) % 4) * WIDE
        return pl.ds(pl.multiple_of(first, WIDE), WIDE)

    def load_col(which, s):
        core = k if which == 0 else 1 - k
        return pltpu.make_async_copy(
            col_hbm.at[:, span(core, s)], col_v.at[which, s], col_sem.at[which, s]
        )

    def load_row(s):
        return pltpu.make_async_copy(
            row_hbm.at[:, span(k, s)], row_v.at[s], row_sem.at[s]
        )

    load_e = pltpu.make_async_copy(e_hbm, e_v, e_sem)
    load_e.start()

    barrier = pltpu.get_barrier_semaphore()
    pl.semaphore_signal(barrier, 1, device_id=sibling, device_id_type=MESH)
    for d in (1, 2, 3):
        for peer in (zpeer(d), xpeer(d), ypeer(d)):
            pl.semaphore_signal(barrier, 1, device_id=peer, device_id_type=MESH)

    def start_loads(s, carry):
        load_col(1, s).start()
        load_col(0, s).start()
        load_row(s).start()
        return carry

    lax.fori_loop(0, STEPS, start_loads, 0)

    home = k * 64 + (y * 4 + x) * 4 + z
    pack[...] = jnp.zeros_like(pack)
    for i in range(CAP):
        pack[i:i + 1, :] = obs_ref[:, i * BLOCK:(i + 1) * BLOCK]
        pack[4 + i:5 + i, :] = noise_ref[:, i * BLOCK:(i + 1) * BLOCK]
    slots[home] = pack[...]

    load_e.wait()
    ef[...] = e_v[...].astype(F32)

    pl.semaphore_wait(barrier, 10)

    quarter = MEMBERS * LROWS // 4
    for piece in range(4):
        for i in range(12):
            at = piece * 12 + i
            plane = ef[pl.ds(at, MEMBERS, stride=LROWS), :]
            esend[at * MEMBERS:(at + 1) * MEMBERS, :] = plane
            lhs[at * MEMBERS:(at + 1) * MEMBERS, 0:LCOLS] = plane.astype(BF16)
        part_rows = pl.ds(piece * quarter, quarter)
        remote(
            esend.at[part_rows], erecv.at[part_rows], es_sem, er_sem.at[piece], sibling
        ).start()

    def send_col(s):
        load_col(1, s).wait()
        csend[s] = col_v[1, s].astype(F32)
        remote(csend.at[s], crecv.at[s], cs_sem, cr_sem.at[s], sibling).start()

    for s in range(AHEAD):
        send_col(s)

    for d in (1, 2, 3):
        remote(slots.at[home], slots.at[home], so, qo_z.at[d - 1], zpeer(d)).start()

    for piece in range(4):
        part_rows = pl.ds(piece * quarter, quarter)
        landed(erecv.at[part_rows], er_sem.at[piece])
        lhs[piece * quarter:(piece + 1) * quarter, LCOLS:2 * LCOLS] = (
            erecv[piece * quarter:(piece + 1) * quarter, :].astype(BF16)
        )
    save_et = pltpu.make_async_copy(lhs.at[:, pl.ds(0, LCOLS)], et_hbm, et_sem)
    save_et.start()

    def compute(s):
        load_col(0, s).wait()
        load_row(s).wait()
        landed(crecv.at[s], cr_sem.at[s])
        rhs[0:LCOLS, :] = col_v[0, s]
        rhs[LCOLS:2 * LCOLS, :] = crecv[s].astype(BF16)
        rowf[...] = row_v[s].astype(F32)
        total = jnp.zeros((MEMBERS, WIDE), F32)
        group = 4
        for g in range(LROWS // group):
            rows = group * MEMBERS
            along = jnp.dot(
                lhs[g * rows:(g + 1) * rows, :], rhs[...], preferred_element_type=F32
            )
            for i in range(group):
                at = g * group + i
                total += along[i * MEMBERS:(i + 1) * MEMBERS] * rowf[at:at + 1, :]
        for q in range(4):
            lanes = slice(q * BLOCK, (q + 1) * BLOCK)
            turn = (q - y + 4) % 4
            pa[s, turn] = total[0:24, lanes]
            pb[s, turn] = total[24:48, lanes]
            pc[s, turn] = total[48:64, lanes]

    def first_sends(w, j):
        s, dz, dx = 4 * w + j, 3 - w, 3 - j

        @pl.when(dz != 0)
        def _():
            remote(
                pa.at[s], ra1.at[dz - 1, j],
                sa.at[0], qa1.at[dz - 1, j], zpeer(dz),
            ).start()

        if dx != 0:
            remote(
                pb.at[s], rb1.at[w, dx - 1],
                sb.at[0], qb1.at[w, dx - 1], xpeer(dx),
            ).start()

        for d in (1, 2, 3):
            remote(
                pc.at[s, d], rc1.at[s, d - 1],
                sc.at[0], qc1.at[s, d - 1], ypeer(d),
            ).start()

    def second_a(w, j):
        s, dz, dx = 4 * w + j, 3 - w, 3 - j

        @pl.when(dz == 0)
        def _():
            for p in range(3):
                landed(ra1.at[p, j], qa1.at[p, j])
            pa[s] = pa[s] + (
                ra1[0, j] + (ra1[1, j] + ra1[2, j])
            )

            if dx != 0:
                remote(
                    pa.at[s], ra2.at[dx - 1],
                    sa.at[1], qa2.at[dx - 1], xpeer(dx),
                ).start()

    def second_b(w, j):
        s, dz, dx = 4 * w + j, 3 - w, 3 - j

        if dx == 0:
            for p in range(3):
                landed(rb1.at[w, p], qb1.at[w, p])
            pb[s] = pb[s] + (rb1[w, 0] + (rb1[w, 1] + rb1[w, 2]))
            for d in (1, 2, 3):
                remote(
                    pb.at[s, d], rb2.at[w, d - 1],
                    sb.at[1], qb2.at[w, d - 1], ypeer(d),
                ).start()

    def second_c(w, j):
        s, dz, dx = 4 * w + j, 3 - w, 3 - j
        for p in range(3):
            landed(rc1.at[s, p], qc1.at[s, p])
        pc[s, 0] = pc[s, 0] + (rc1[s, 0] + (rc1[s, 1] + rc1[s, 2]))

        @pl.when(dz != 0)
        def _():
            remote(
                pc.at[s, 0], rc2.at[dz - 1, j],
                sc.at[1], qc2.at[dz - 1, j], zpeer(dz),
            ).start()

    def third_a():
        s = STEPS - 1
        for p in range(3):
            landed(ra2.at[p], qa2.at[p])
        pa[s] = pa[s] + (ra2[0] + (ra2[1] + ra2[2]))
        for d in (1, 2, 3):
            remote(
                pa.at[s, d], ra3.at[d - 1],
                sa.at[2], qa3.at[d - 1], ypeer(d),
            ).start()

    def third_b(w, j):
        s, dz, dx = 4 * w + j, 3 - w, 3 - j

        if dx == 0:
            for p in range(3):
                landed(rb2.at[w, p], qb2.at[w, p])
            pb[s, 0] = pb[s, 0] + (rb2[w, 0] + (rb2[w, 1] + rb2[w, 2]))

            @pl.when(dz != 0)
            def _():
                remote(
                    pb.at[s, 0], rb3.at[dz - 1],
                    sb.at[2], qb3.at[dz - 1], zpeer(dz),
                ).start()

    def third_c(w, j):
        s, dz, dx = 4 * w + j, 3 - w, 3 - j

        @pl.when(dz == 0)
        def _():
            for p in range(3):
                landed(rc2.at[p, j], qc2.at[p, j])
            pc[s, 0] = pc[s, 0] + (
                rc2[0, j] + (rc2[1, j] + rc2[2, j])
            )

            if dx != 0:
                remote(
                    pc.at[s, 0], rc3.at[dx - 1],
                    sc.at[2], qc3.at[dx - 1], xpeer(dx),
                ).start()

    base_x = k * 64 + (y * 4 + x) * 4
    base_y = k * 64 + y * 16
    base_k = k * 64

    def slots_x():
        for d in (1, 2, 3):
            landed(slots.at[home], qo_z.at[d - 1])
        mine = slots.at[pl.ds(base_x, 4)]
        for d in (1, 2, 3):
            remote(mine, mine, so, qo_x.at[d - 1], xpeer(d)).start()

    def slots_y():
        for d in (1, 2, 3):
            landed(slots.at[pl.ds(base_x, 4)], qo_x.at[d - 1])
        mine = slots.at[pl.ds(base_y, 16)]
        for d in (1, 2, 3):
            remote(mine, mine, so, qo_y.at[d - 1], ypeer(d)).start()

    def slots_k():
        for d in (1, 2, 3):
            landed(slots.at[pl.ds(base_y, 16)], qo_y.at[d - 1])
        mine = slots.at[pl.ds(base_k, 64)]
        remote(mine, mine, so, qo_k, sibling).start()

    def lagged(events, w, j, lag):
        back = (j - lag) // 4
        late, at = w + back, (j - lag) % 4

        def run():
            for event in events:
                event(late, at)

        if back == 0:
            run()
        else:
            pl.when(late >= 0)(run)

    def phase(w, carry):
        for j in range(4):
            s = 4 * w + j
            pl.when(s + AHEAD < STEPS)(functools.partial(send_col, s + AHEAD))
            compute(s)
            first_sends(w, j)
            lagged((second_a, second_b, second_c), w, j, LAG2)
            lagged((third_b, third_c), w, j, LAG3)
        pl.when(w == 0)(slots_x)
        pl.when(w == 1)(slots_y)
        pl.when(w == 2)(slots_k)
        return carry

    lax.fori_loop(0, STEPS // 4, phase, 0)

    last = STEPS - 1
    for s in range(STEPS - LAG2, last):
        second_a(s // 4, s % 4)
        second_b(s // 4, s % 4)
        second_c(s // 4, s % 4)
    for s in range(STEPS - LAG3, last):
        third_b(s // 4, s % 4)
        third_c(s // 4, s % 4)
    second_a(3, 3)
    second_b(3, 3)
    third_a()
    second_c(3, 3)
    third_c(3, 3)
    third_b(3, 3)

    landed(slots.at[pl.ds(base_k, 64)], qo_k)
    me = ((k * 4 + z) * 4 + x) * 4 + y
    owner = owner_ref[me]

    def count(b, n):
        return n + jnp.where(jnp.logical_and(owner_ref[b] == owner, b < me), 1, 0)

    rank = lax.fori_loop(0, owner_ref.shape[0], count, jnp.int32(0))
    o_row, o_col = owner // 8, owner % 8
    found = slots[(o_col % 2) * 64 + o_row * 4 + o_col // 2]
    observed = jnp.where(
        rank == 0, found[0:1], jnp.where(rank == 1, found[1:2], found[2:3])
    )
    variance = jnp.where(
        rank == 0, found[4:5], jnp.where(rank == 1, found[5:6], found[6:7])
    )
    weight = 1.0 / variance

    for d in range(3):
        landed(ra3.at[d], qa3.at[d])
        landed(rb3.at[d], qb3.at[d])
        landed(rc3.at[d], qc3.at[d])
    predictions = jnp.concatenate(
        [
            pa[last, 0] + (ra3[0] + (ra3[1] + ra3[2])),
            pb[last, 0] + (rb3[0] + (rb3[1] + rb3[2])),
            pc[last, 0] + (rc3[0] + (rc3[1] + rc3[2])),
        ],
        axis=0,
    )
    mean = jnp.mean(predictions, axis=0, keepdims=True)
    anomalies = (predictions - mean) * (1.0 / ROOT)
    scaled = anomalies * weight
    offset = jnp.where(
        lax.broadcasted_iota(jnp.int32, (8, BLOCK), 0) == 0, observed - mean, 0.0
    )
    blank = jnp.zeros((8, BLOCK), F32)
    left = jnp.concatenate([anomalies[0:16], anomalies[32:48], offset], axis=0)
    right = jnp.concatenate([anomalies[16:32], anomalies[48:64], blank], axis=0)
    none = jnp.zeros((MEMBERS, BLOCK), F32)
    contract = (((1,), (1,)), ((), ()))
    packed = lax.dot_general(
        left, jnp.concatenate([scaled, none], axis=0), contract,
        precision=lax.Precision.HIGHEST, preferred_element_type=F32,
    ) + lax.dot_general(
        right, jnp.concatenate([none, scaled], axis=0), contract,
        precision=lax.Precision.HIGHEST, preferred_element_type=F32,
    )
    got[0, 0, 0:16] = packed[0:16]
    got[0, 0, 16:24] = packed[32:40]
    got[0, 1, 0:16] = packed[16:32]
    got[0, 1, 16:24] = jnp.zeros((8, BLOCK), F32)

    remote(got.at[0, 1 - k], got_core.at[0], st.at[0], qt.at[0], sibling).start()
    landed(got_core.at[0], qt.at[0])
    got[1, 0] = got[0, k] + got_core[0]
    for stage, peers in enumerate((zpeer, xpeer, ypeer)):
        for d in (1, 2, 3):
            remote(
                got.at[1 + stage, 0], got_core.at[1 + 3 * stage + d - 1],
                st.at[1 + 3 * stage + d - 1], qt.at[1 + 3 * stage + d - 1], peers(d),
            ).start()
        for d in (1, 2, 3):
            landed(got_core.at[1 + 3 * stage + d - 1], qt.at[1 + 3 * stage + d - 1])
        first = 1 + 3 * stage
        total = got[1 + stage, 0] + (
            got_core[first] + (got_core[first + 1] + got_core[first + 2])
        )
        got[2 + stage, 0] = total
    remote(got.at[4, 0], got_core.at[10], st.at[10], qt.at[10], sibling).start()
    sums_ref[k] = got[4, 0]
    landed(got_core.at[10], qt.at[10])
    sums_ref[1 - k] = got_core[10]

    save_et.wait()
    sent(esend, es_sem)
    sent(csend, cs_sem)
    sent(pa.at[pl.ds(0, 12), :], sa.at[0])
    sent(pa.at[pl.ds(0, 3), :], sa.at[1])
    sent(pa.at[0, pl.ds(0, 3)], sa.at[2])
    sent(pb.at[pl.ds(0, 12), :], sb.at[0])
    sent(pb.at[pl.ds(0, 4), pl.ds(0, 3)], sb.at[1])
    sent(pb.at[0, pl.ds(0, 3)], sb.at[2])
    sent(pc.at[pl.ds(0, 16), pl.ds(0, 3)], sc.at[0])
    sent(pc.at[pl.ds(0, 12), 0], sc.at[1])
    sent(pc.at[0, pl.ds(0, 3)], sc.at[2])
    sent(slots.at[pl.ds(0, 3 + 12 + 48 + 64)], so)
    for i in range(11):
        sent(got_core.at[0], st.at[i])


def apply_kernel(sums_ref, et_ref, out_ref, full):
    low = sums_ref[0, 0:16]
    high = sums_ref[1, 0:16]
    spread = jnp.concatenate(
        [low, pltpu.roll(low, 64, 1), high, pltpu.roll(high, 64, 1)], axis=0
    )
    r_row = sums_ref[0, 16:17] + sums_ref[1, 16:17]
    row_at = lax.broadcasted_iota(jnp.int32, (MEMBERS, 2 * MEMBERS), 0)
    lane_at = lax.broadcasted_iota(jnp.int32, (MEMBERS, 2 * MEMBERS), 1)
    left = lane_at < MEMBERS
    eye = jnp.where(row_at == lane_at, 1.0, 0.0)
    grid = jnp.where(left, spread + eye, jnp.where(lane_at - MEMBERS == row_at, 1.0, 0.0))
    for p in range(MEMBERS):
        pivot_row = grid[p:p + 1, :]
        scaled = pivot_row / pivot_row[:, p:p + 1]
        grid = jnp.where(row_at == p, scaled, grid - grid[:, p:p + 1] * scaled)
    inverse = jnp.where(left, pltpu.roll(grid, 64, 1), 0.0)
    r_col = jnp.sum(jnp.where(row_at == lane_at, r_row, 0.0), axis=1, keepdims=True)
    shift = jnp.sum(inverse * r_col, axis=0, keepdims=True)
    gain_t = jnp.where(left, shift - ROOT * (eye - inverse), 0.0)
    centre = jnp.sum(gain_t, axis=1, keepdims=True) * (1.0 / MEMBERS)
    moves = jnp.where(left, (gain_t - centre) * (1.0 / ROOT), 0.0)
    one = moves.astype(BF16).astype(F32)
    two = (moves - one).astype(BF16).astype(F32)
    three = moves - one - two
    factors = jnp.concatenate(
        [(one + pltpu.roll(two, 64, 1)).astype(BF16), three.astype(BF16)], axis=1
    )[:, 0:2 * BLOCK]
    zero = jnp.zeros((MEMBERS, 2 * BLOCK), BF16)
    for g in range(LROWS // 2):
        at = 2 * g * MEMBERS
        pair = jnp.concatenate(
            [et_ref[at:at + MEMBERS, :], et_ref[at + MEMBERS:at + 2 * MEMBERS, :]], axis=1
        )
        moved = pair.astype(F32) + jnp.dot(
            factors, jnp.concatenate([pair, pair, pair, zero], axis=0),
            preferred_element_type=F32,
        )
        full[pl.ds(2 * g, MEMBERS, stride=LROWS), :] = moved[:, 0:BLOCK]
        full[pl.ds(2 * g + 1, MEMBERS, stride=LROWS), :] = moved[:, BLOCK:2 * BLOCK]
    out_ref[...] = full[...].astype(BF16)


def on_device(ensemble, row_profile, col_profile, obs_owned, noise_owned, block_owner):
    field = ensemble.reshape(MEMBERS * LROWS, LCOLS)
    hbm = pl.BlockSpec(memory_space=pltpu.HBM)
    vmem = pl.BlockSpec(memory_space=pltpu.VMEM)
    smem = pl.BlockSpec(memory_space=pltpu.SMEM)
    dma = pltpu.SemaphoreType.DMA
    size = MEMBERS * LROWS
    sums, field_t = pl.pallas_call(
        partial_kernel,
        name="partial_sums",
        out_shape=(
            jax.ShapeDtypeStruct((2, 24, BLOCK), F32),
            jax.ShapeDtypeStruct((size, LCOLS), BF16),
        ),
        in_specs=[hbm, hbm, hbm, vmem, vmem, smem],
        out_specs=(vmem, hbm),
        scratch_shapes=[
            pltpu.VMEM((size, LCOLS), BF16),
            pltpu.VMEM((size, LCOLS), F32),
            pltpu.VMEM((size, LCOLS), F32),
            pltpu.VMEM((size, LCOLS), F32),
            pltpu.VMEM((size, 2 * LCOLS), BF16),
            pltpu.VMEM((2, STEPS, LCOLS, WIDE), BF16),
            pltpu.VMEM((STEPS, LROWS, WIDE), BF16),
            pltpu.VMEM((STEPS, LCOLS, WIDE), F32),
            pltpu.VMEM((STEPS, LCOLS, WIDE), F32),
            pltpu.VMEM((2 * LCOLS, WIDE), BF16),
            pltpu.VMEM((LROWS, WIDE), F32),
            pltpu.VMEM((STEPS, 4, 24, BLOCK), F32),
            pltpu.VMEM((STEPS, 4, 24, BLOCK), F32),
            pltpu.VMEM((STEPS, 4, 16, BLOCK), F32),
            pltpu.VMEM((3, 4, 4, 24, BLOCK), F32),
            pltpu.VMEM((3, 4, 24, BLOCK), F32),
            pltpu.VMEM((3, 24, BLOCK), F32),
            pltpu.VMEM((4, 3, 4, 24, BLOCK), F32),
            pltpu.VMEM((4, 3, 24, BLOCK), F32),
            pltpu.VMEM((3, 24, BLOCK), F32),
            pltpu.VMEM((STEPS, 3, 16, BLOCK), F32),
            pltpu.VMEM((3, 4, 16, BLOCK), F32),
            pltpu.VMEM((3, 16, BLOCK), F32),
            pltpu.VMEM((128, 8, BLOCK), F32),
            pltpu.VMEM((8, BLOCK), F32),
            pltpu.VMEM((11, 24, BLOCK), F32),
            pltpu.VMEM((5, 2, 24, BLOCK), F32),
            dma, dma, dma((2, STEPS)), dma((STEPS,)),
            dma, dma((4,)), dma, dma((STEPS,)),
            dma((3,)), dma((3,)), dma((3,)),
            dma((3, 4)), dma((3,)), dma((3,)),
            dma((4, 3)), dma((4, 3)), dma((3,)),
            dma((STEPS, 3)), dma((3, 4)), dma((3,)),
            dma, dma((3,)), dma((3,)), dma((3,)), dma,
            dma((11,)), dma((11,)),
        ],
        compiler_params=pltpu.CompilerParams(
            collective_id=0, has_side_effects=True, vmem_limit_bytes=48 << 20
        ),
    )(field, col_profile, row_profile, obs_owned, noise_owned, block_owner)
    moved = pl.pallas_call(
        apply_kernel,
        name="solve_apply",
        out_shape=jax.ShapeDtypeStruct((size, LCOLS), BF16),
        in_specs=[vmem, vmem],
        out_specs=vmem,
        scratch_shapes=[pltpu.VMEM((size, LCOLS), F32)],
        compiler_params=pltpu.CompilerParams(vmem_limit_bytes=32 << 20),
    )(sums, field_t)
    return moved.reshape(ensemble.shape)


def solution(mesh):
    in_specs = (
        P(None, "rows", "cols"),
        P("rows", None),
        P("cols", None),
        P(("rows", "cols"), None),
        P(("rows", "cols"), None),
        P(),
    )
    return jax.shard_map(
        on_device, mesh=mesh, in_specs=in_specs, out_specs=P(None, "rows", "cols"),
        check_vma=False,
    )
```

```python
import functools
import math

import jax
import jax.numpy as jnp
from jax import lax
from jax.experimental import pallas as pl
from jax.experimental.pallas import tpu as pltpu
from jax.sharding import PartitionSpec as P

MEMBERS = 64
BLOCK = 128
CAP = 3
LROWS = 48
LCOLS = 128
STEPS = 16
WIDE = 512
AHEAD = 3
LAG2 = 3
LAG3 = 6
ROOT = math.sqrt(MEMBERS - 1)
MESH = pl.DeviceIdType.MESH
F32 = jnp.float32
BF16 = jnp.bfloat16


def here():
    r = lax.axis_index("rows")
    c = lax.axis_index("cols")
    return r // 4, r % 4, c // 2, c % 2


def device(y, x, z, k):
    return (y * 4 + x, z * 2 + k)


def partial_kernel(
    e_hbm, col_hbm, row_hbm, obs_hbm, noise_hbm, owner_hbm,
    sums_ref, et_hbm,
    e_v, ef, esend, erecv, lhs, col_v, row_v, csend, crecv, rhs, rowf, pa, pb, pc,
    ra1, ra2, ra3, rb1, rb2, rb3, rc1, rc2, rc3, slots, pack, got_core, got,
    obs_ref, noise_ref, owner_ref, owner_row, small_sem,
    e_sem, et_sem, col_sem, row_sem,
    es_sem, er_sem, cs_sem, cr_sem,
    sa, sb, sc,
    qa1, qa2, qa3, qb1, qb2, qb3, qc1, qc2, qc3,
    so, qo_z, qo_x, qo_y, qo_k,
    st, qt,
):
    y, x, z, k = here()
    sibling = device(y, x, z, 1 - k)
    turn = 1 - 2 * k

    def zpeer(d):
        return device(y, x, (z + turn * d + 4) % 4, k)

    def xpeer(d):
        return device(y, (x + turn * d + 4) % 4, z, k)

    def ypeer(d):
        return device((y + turn * d + 4) % 4, x, z, k)

    def flat(d):
        return device((y + d // 4) % 4, (x + d % 4) % 4, z, k)

    def remote(src, dst, send, recv, to):
        return pltpu.make_async_remote_copy(
            src_ref=src, dst_ref=dst, send_sem=send, recv_sem=recv,
            device_id=to, device_id_type=MESH,
        )

    def sent(src, sem):
        remote(src, src, sem, sem, sibling).wait_send()

    def landed(dst, sem):
        remote(dst, dst, sem, sem, sibling).wait_recv()

    def span(core, s):
        dz, dx = 3 - s // 4, 3 - s % 4
        way = 1 - 2 * core
        to_z, to_x = (z + way * dz + 4) % 4, (x + way * dx + 4) % 4
        first = ((core * 4 + to_z) * 4 + to_x) * WIDE
        return pl.ds(pl.multiple_of(first, WIDE), WIDE)

    def load_col(which, s):
        core = k if which == 0 else 1 - k
        return pltpu.make_async_copy(
            col_hbm.at[:, span(core, s)], col_v.at[which, s], col_sem.at[which, s]
        )

    def load_row(s):
        return pltpu.make_async_copy(
            row_hbm.at[:, span(k, s)], row_v.at[s], row_sem.at[s]
        )

    load_e = pltpu.make_async_copy(e_hbm, e_v, e_sem)
    load_e.start()
    load_small = [
        pltpu.make_async_copy(src, dst, small_sem.at[i])
        for i, (src, dst) in enumerate(
            ((obs_hbm, obs_ref), (noise_hbm, noise_ref), (owner_hbm, owner_ref),
             (owner_hbm, owner_row))
        )
    ]
    for load in load_small:
        load.start()

    barrier = pltpu.get_barrier_semaphore()
    pl.semaphore_signal(barrier, 1, device_id=sibling, device_id_type=MESH)
    for peer in [zpeer(d) for d in (1, 2, 3)] + [flat(d) for d in range(1, 16)]:
        pl.semaphore_signal(barrier, 1, device_id=peer, device_id_type=MESH)

    def start_loads(s, carry):
        load_col(1, s).start()
        load_col(0, s).start()
        load_row(s).start()
        return carry

    lax.fori_loop(0, STEPS, start_loads, 0)

    home = k * 64 + (y * 4 + x) * 4 + z
    pack[...] = jnp.zeros_like(pack)
    for load in load_small:
        load.wait()
    for i in range(CAP):
        pack[i:i + 1, :] = obs_ref[:, i * BLOCK:(i + 1) * BLOCK]
        pack[4 + i:5 + i, :] = noise_ref[:, i * BLOCK:(i + 1) * BLOCK]
    slots[home] = pack[...]

    load_e.wait()
    ef[...] = e_v[...].astype(F32)

    pl.semaphore_wait(barrier, 19)

    quarter = MEMBERS * LROWS // 4
    for piece in range(4):
        for i in range(12):
            at = piece * 12 + i
            plane = ef[pl.ds(at, MEMBERS, stride=LROWS), :]
            esend[at * MEMBERS:(at + 1) * MEMBERS, :] = plane
            lhs[at * MEMBERS:(at + 1) * MEMBERS, 0:LCOLS] = plane.astype(BF16)
        part_rows = pl.ds(piece * quarter, quarter)
        remote(
            esend.at[part_rows], erecv.at[part_rows], es_sem, er_sem.at[piece], sibling
        ).start()

    def send_col(s):
        load_col(1, s).wait()
        csend[s] = col_v[1, s].astype(F32)
        remote(csend.at[s], crecv.at[s], cs_sem, cr_sem.at[s], sibling).start()

    for s in range(AHEAD):
        send_col(s)

    for d in (1, 2, 3):
        remote(slots.at[home], slots.at[home], so, qo_z.at[d - 1], zpeer(d)).start()

    for piece in range(4):
        part_rows = pl.ds(piece * quarter, quarter)
        landed(erecv.at[part_rows], er_sem.at[piece])
        lhs[piece * quarter:(piece + 1) * quarter, LCOLS:2 * LCOLS] = (
            erecv[piece * quarter:(piece + 1) * quarter, :].astype(BF16)
        )
    save_et = pltpu.make_async_copy(lhs.at[:, pl.ds(0, LCOLS)], et_hbm, et_sem)
    save_et.start()

    def compute(s):
        load_col(0, s).wait()
        load_row(s).wait()
        landed(crecv.at[s], cr_sem.at[s])
        rhs[0:LCOLS, :] = col_v[0, s]
        rhs[LCOLS:2 * LCOLS, :] = crecv[s].astype(BF16)
        rowf[...] = row_v[s].astype(F32)
        total = jnp.zeros((MEMBERS, WIDE), F32)
        group = 4
        for g in range(LROWS // group):
            rows = group * MEMBERS
            along = jnp.dot(
                lhs[g * rows:(g + 1) * rows, :], rhs[...], preferred_element_type=F32
            )
            for i in range(group):
                at = g * group + i
                total += along[i * MEMBERS:(i + 1) * MEMBERS] * rowf[at:at + 1, :]
        for q in range(4):
            lanes = slice(q * BLOCK, (q + 1) * BLOCK)
            place = (turn * (q - y) + 4) % 4
            pa[s, place] = total[0:24, lanes]
            pb[s, place] = total[24:40, lanes]
            pc[s, place] = total[40:64, lanes]

    def first_sends(w, j):
        s, dz, dx = 4 * w + j, 3 - w, 3 - j

        @pl.when(dz != 0)
        def _():
            remote(
                pa.at[s], ra1.at[dz - 1, j],
                sa.at[0], qa1.at[dz - 1, j], zpeer(dz),
            ).start()

        if dx != 0:
            remote(
                pb.at[s], rb1.at[w, dx - 1],
                sb.at[0], qb1.at[w, dx - 1], xpeer(dx),
            ).start()

        for d in (1, 2, 3):
            remote(
                pc.at[s, d], rc1.at[s, d - 1],
                sc.at[0], qc1.at[s, d - 1], ypeer(d),
            ).start()

    def second_a(w, j):
        s, dz, dx = 4 * w + j, 3 - w, 3 - j

        @pl.when(dz == 0)
        def _():
            for p in range(3):
                landed(ra1.at[p, j], qa1.at[p, j])
            pa[s] = pa[s] + (
                ra1[0, j] + (ra1[1, j] + ra1[2, j])
            )

            if dx != 0:
                remote(
                    pa.at[s], ra2.at[dx - 1],
                    sa.at[1], qa2.at[dx - 1], xpeer(dx),
                ).start()

    def second_b(w, j):
        s, dz, dx = 4 * w + j, 3 - w, 3 - j

        if dx == 0:
            for p in range(3):
                landed(rb1.at[w, p], qb1.at[w, p])
            pb[s] = pb[s] + (rb1[w, 0] + (rb1[w, 1] + rb1[w, 2]))
            for d in (1, 2, 3):
                remote(
                    pb.at[s, d], rb2.at[w, d - 1],
                    sb.at[1], qb2.at[w, d - 1], ypeer(d),
                ).start()

    def second_c(w, j):
        s, dz, dx = 4 * w + j, 3 - w, 3 - j
        for p in range(3):
            landed(rc1.at[s, p], qc1.at[s, p])
        pc[s, 0] = pc[s, 0] + (rc1[s, 0] + (rc1[s, 1] + rc1[s, 2]))

        @pl.when(dz != 0)
        def _():
            remote(
                pc.at[s, 0], rc2.at[dz - 1, j],
                sc.at[1], qc2.at[dz - 1, j], zpeer(dz),
            ).start()

    def third_a():
        s = STEPS - 1
        for p in range(3):
            landed(ra2.at[p], qa2.at[p])
        pa[s] = pa[s] + (ra2[0] + (ra2[1] + ra2[2]))
        for d in (1, 2, 3):
            remote(
                pa.at[s, d], ra3.at[d - 1],
                sa.at[2], qa3.at[d - 1], ypeer(d),
            ).start()

    def third_b(w, j):
        s, dz, dx = 4 * w + j, 3 - w, 3 - j

        if dx == 0:
            for p in range(3):
                landed(rb2.at[w, p], qb2.at[w, p])
            pb[s, 0] = pb[s, 0] + (rb2[w, 0] + (rb2[w, 1] + rb2[w, 2]))

            @pl.when(dz != 0)
            def _():
                remote(
                    pb.at[s, 0], rb3.at[dz - 1],
                    sb.at[2], qb3.at[dz - 1], zpeer(dz),
                ).start()

    def third_c(w, j):
        s, dz, dx = 4 * w + j, 3 - w, 3 - j

        @pl.when(dz == 0)
        def _():
            for p in range(3):
                landed(rc2.at[p, j], qc2.at[p, j])
            pc[s, 0] = pc[s, 0] + (
                rc2[0, j] + (rc2[1, j] + rc2[2, j])
            )

            if dx != 0:
                remote(
                    pc.at[s, 0], rc3.at[dx - 1],
                    sc.at[2], qc3.at[dx - 1], xpeer(dx),
                ).start()

    base_x = k * 64 + (y * 4 + x) * 4
    base_y = k * 64 + y * 16
    base_k = k * 64

    def slots_x():
        for d in (1, 2, 3):
            landed(slots.at[home], qo_z.at[d - 1])
        mine = slots.at[pl.ds(base_x, 4)]
        for d in (1, 2, 3):
            remote(mine, mine, so, qo_x.at[d - 1], xpeer(d)).start()

    def slots_y():
        for d in (1, 2, 3):
            landed(slots.at[pl.ds(base_x, 4)], qo_x.at[d - 1])
        mine = slots.at[pl.ds(base_y, 16)]
        for d in (1, 2, 3):
            remote(mine, mine, so, qo_y.at[d - 1], ypeer(d)).start()

    def slots_k():
        for d in (1, 2, 3):
            landed(slots.at[pl.ds(base_y, 16)], qo_y.at[d - 1])
        mine = slots.at[pl.ds(base_k, 64)]
        remote(mine, mine, so, qo_k, sibling).start()

    def lagged(events, w, j, lag):
        back = (j - lag) // 4
        late, at = w + back, (j - lag) % 4

        def run():
            for event in events:
                event(late, at)

        if back == 0:
            run()
        else:
            pl.when(late >= 0)(run)

    def phase(w, carry):
        for j in range(4):
            s = 4 * w + j
            pl.when(s + AHEAD < STEPS)(functools.partial(send_col, s + AHEAD))
            compute(s)
            first_sends(w, j)
            second_a(w, j)
            lagged((second_b, second_c), w, j, LAG2)
            lagged((third_b, third_c), w, j, LAG3)
        pl.when(w == 0)(slots_x)
        pl.when(w == 1)(slots_y)
        pl.when(w == 2)(slots_k)
        return carry

    lax.fori_loop(0, STEPS // 4, phase, 0)

    last = STEPS - 1
    third_b(2, 3)
    second_c(3, 1)
    third_c(3, 0)
    third_c(3, 1)
    second_c(3, 2)
    third_c(3, 2)
    second_b(3, 3)
    third_a()
    second_c(3, 3)
    third_c(3, 3)
    third_b(3, 3)

    landed(slots.at[pl.ds(base_k, 64)], qo_k)
    me = ((k * 4 + z) * 4 + x) * 4 + y
    owner = owner_ref[0, me]
    owners = owner_row[...]
    block_at = lax.broadcasted_iota(jnp.int32, (1, BLOCK), 1)
    before = jnp.logical_and(owners == owner, block_at < me)
    rank = jnp.sum(jnp.where(before, 1.0, 0.0), axis=1, keepdims=True)
    o_row, o_col = owner // 8, owner % 8
    found = slots[(o_col % 2) * 64 + o_row * 4 + o_col // 2]
    observed = jnp.where(
        rank < 0.5, found[0:1], jnp.where(rank < 1.5, found[1:2], found[2:3])
    )
    variance = jnp.where(
        rank < 0.5, found[4:5], jnp.where(rank < 1.5, found[5:6], found[6:7])
    )
    weight = 1.0 / variance

    for d in range(3):
        landed(ra3.at[d], qa3.at[d])
        landed(rb3.at[d], qb3.at[d])
        landed(rc3.at[d], qc3.at[d])
    predictions = jnp.concatenate(
        [
            pa[last, 0] + (ra3[0] + (ra3[1] + ra3[2])),
            pb[last, 0] + (rb3[0] + (rb3[1] + rb3[2])),
            pc[last, 0] + (rc3[0] + (rc3[1] + rc3[2])),
        ],
        axis=0,
    )
    mean = jnp.mean(predictions, axis=0, keepdims=True)
    anomalies = (predictions - mean) * (1.0 / ROOT)
    scaled = anomalies * weight
    target = anomalies + (observed - mean)
    blank = jnp.zeros((MEMBERS, BLOCK), F32)
    contract = (((1,), (1,)), ((), ()))
    left = jnp.concatenate([scaled[0:16], scaled[32:48]], axis=0)
    right = jnp.concatenate([scaled[16:32], scaled[48:64]], axis=0)
    packed = lax.dot_general(
        left, jnp.concatenate([target, blank], axis=0), contract,
        precision=lax.Precision.HIGHEST, preferred_element_type=F32,
    ) + lax.dot_general(
        right, jnp.concatenate([blank, target], axis=0), contract,
        precision=lax.Precision.HIGHEST, preferred_element_type=F32,
    )
    got[0, 0] = packed[0:16]
    got[0, 1] = packed[16:32]

    remote(got.at[0, 1 - k], got_core.at[0], st.at[0], qt.at[0], sibling).start()
    landed(got_core.at[0], qt.at[0])
    got[1, 0] = got[0, k] + got_core[0]
    for d in (1, 2, 3):
        remote(
            got.at[1, 0], got_core.at[d], st.at[d], qt.at[d], zpeer(d)
        ).start()
    for d in (1, 2, 3):
        landed(got_core.at[d], qt.at[d])
    got[2, 0] = got[1, 0] + (got_core[1] + (got_core[2] + got_core[3]))
    for d in range(1, 16):
        remote(
            got.at[2, 0], got_core.at[3 + d], st.at[3 + d], qt.at[3 + d], flat(d)
        ).start()
    total = got[2, 0]
    for d in range(1, 16):
        landed(got_core.at[3 + d], qt.at[3 + d])
        total += got_core[3 + d]
    got[3, 0] = total
    end = 19
    whole = 3
    remote(got.at[whole, 0], got_core.at[end], st.at[end], qt.at[end], sibling).start()
    sums_ref[k] = got[whole, 0]
    landed(got_core.at[end], qt.at[end])
    sums_ref[1 - k] = got_core[end]

    save_et.wait()
    sent(esend, es_sem)
    sent(csend, cs_sem)
    sent(pa.at[pl.ds(0, 12), :], sa.at[0])
    sent(pa.at[pl.ds(0, 3), :], sa.at[1])
    sent(pa.at[0, pl.ds(0, 3)], sa.at[2])
    sent(pb.at[pl.ds(0, 12), :], sb.at[0])
    sent(pb.at[pl.ds(0, 4), pl.ds(0, 3)], sb.at[1])
    sent(pb.at[0, pl.ds(0, 3)], sb.at[2])
    sent(pc.at[pl.ds(0, 16), pl.ds(0, 3)], sc.at[0])
    sent(pc.at[pl.ds(0, 12), 0], sc.at[1])
    sent(pc.at[0, pl.ds(0, 3)], sc.at[2])
    sent(slots.at[pl.ds(0, 3 + 12 + 48 + 64)], so)
    for i in range(20):
        sent(got_core.at[0], st.at[i])


def lane(panel, at):
    return jnp.broadcast_to(panel[:, at:at + 1], panel.shape)


def sub(panel, at):
    return jnp.broadcast_to(panel[at:at + 1], panel.shape)


def pivot_four(panel, column, t):
    at = lax.broadcasted_iota(jnp.int32, panel.shape, 0)
    c = [lane(panel, column + t + i) for i in range(4)]
    r = [sub(panel, t + i) for i in range(4)]
    a, q, d = sub(c[0], t), sub(c[0], t + 1), sub(c[1], t + 1)
    e00, e01, e10, e11 = (
        sub(c[0], t + 2), sub(c[1], t + 2), sub(c[0], t + 3), sub(c[1], t + 3)
    )
    f, g, h = sub(c[2], t + 2), sub(c[2], t + 3), sub(c[3], t + 3)
    inv = 1.0 / (a * d - q * q)
    w00, w01 = (e00 * d - e01 * q) * inv, (e01 * a - e00 * q) * inv
    w10, w11 = (e10 * d - e11 * q) * inv, (e11 * a - e10 * q) * inv
    f = f - (w00 * e00 + w01 * e01)
    g = g - (w00 * e10 + w01 * e11)
    h = h - (w10 * e10 + w11 * e11)
    rest = 1.0 / (f * h - g * g)
    u = r[2] - (w00 * r[0] + w01 * r[1])
    v = r[3] - (w10 * r[0] + w11 * r[1])
    n2, n3 = (h * u - g * v) * rest, (f * v - g * u) * rest
    n0 = (d * r[0] - q * r[1]) * inv - (w00 * n2 + w10 * n3)
    n1 = (a * r[1] - q * r[0]) * inv - (w01 * n2 + w11 * n3)
    new = panel - ((c[0] * n0 + c[1] * n1) + (c[2] * n2 + c[3] * n3))
    for i, row in enumerate((n0, n1, n2, n3)):
        new = jnp.where(at == t + i, row, new)
    return new


def eliminate(grid):
    panels = [grid[8 * i:8 * i + 8] for i in range(8)]
    for b in range(8):
        columns = [
            [lane(panels[i], 8 * b + t) for t in range(8)] if i != b else None
            for i in range(8)
        ]
        done = pivot_four(pivot_four(panels[b], 8 * b, 0), 8 * b, 4)
        rows = [sub(done, t) for t in range(8)]
        for i in range(8):
            if i != b:
                m = [columns[i][t] * rows[t] for t in range(8)]
                panels[i] = panels[i] - (
                    ((m[0] + m[1]) + (m[2] + m[3])) + ((m[4] + m[5]) + (m[6] + m[7]))
                )
        panels[b] = done
    return jnp.concatenate(panels, axis=0)


def apply_kernel(sums_ref, et_hbm, out_ref, full, et_ref, et_sem):
    load = pltpu.make_async_copy(et_hbm, et_ref, et_sem)
    load.start()
    low, high = sums_ref[0], sums_ref[1]
    both = jnp.concatenate(
        [low, pltpu.roll(low, 64, 1), high, pltpu.roll(high, 64, 1)], axis=0
    )
    row_at = lax.broadcasted_iota(jnp.int32, (MEMBERS, 2 * MEMBERS), 0)
    lane_at = lax.broadcasted_iota(jnp.int32, (MEMBERS, 2 * MEMBERS), 1)
    left = lane_at < MEMBERS
    r_col = jnp.sum(jnp.where(left, both, 0.0), axis=1, keepdims=True) * (1.0 / MEMBERS)
    eye = jnp.where(row_at == lane_at, 1.0, 0.0)
    grid = eliminate(
        jnp.where(
            left, (both - r_col) + eye, jnp.where(lane_at - MEMBERS == row_at, 1.0, 0.0)
        )
    )
    inverse = jnp.where(left, pltpu.roll(grid, 64, 1), 0.0)
    shift = jnp.sum(inverse * r_col, axis=0, keepdims=True)
    gain_t = jnp.where(left, shift - ROOT * (eye - inverse), 0.0)
    centre = jnp.sum(gain_t, axis=1, keepdims=True) * (1.0 / MEMBERS)
    moves = jnp.where(left, (gain_t - centre) * (1.0 / ROOT), 0.0)
    one = moves.astype(BF16).astype(F32)
    two = (moves - one).astype(BF16).astype(F32)
    three = moves - one - two
    factors = jnp.concatenate(
        [(one + pltpu.roll(two, 64, 1)).astype(BF16), three.astype(BF16)], axis=1
    )
    zero = jnp.zeros((MEMBERS, 2 * BLOCK), BF16)
    load.wait()
    for g in range(LROWS // 2):
        at = 2 * g * MEMBERS
        pair = jnp.concatenate(
            [et_ref[at:at + MEMBERS, :], et_ref[at + MEMBERS:at + 2 * MEMBERS, :]], axis=1
        )
        moved = pair.astype(F32) + jnp.dot(
            factors, jnp.concatenate([pair, pair, pair, zero], axis=0),
            preferred_element_type=F32,
        )
        full[pl.ds(2 * g, MEMBERS, stride=LROWS), :] = moved[:, 0:BLOCK]
        full[pl.ds(2 * g + 1, MEMBERS, stride=LROWS), :] = moved[:, BLOCK:2 * BLOCK]
    out_ref[...] = full[...].astype(BF16)


def on_device(ensemble, row_profile, col_profile, obs_owned, noise_owned, block_owner):
    field = ensemble.reshape(MEMBERS * LROWS, LCOLS)
    hbm = pl.BlockSpec(memory_space=pltpu.HBM)
    vmem = pl.BlockSpec(memory_space=pltpu.VMEM)
    dma = pltpu.SemaphoreType.DMA
    size = MEMBERS * LROWS
    sums, field_t = pl.pallas_call(
        partial_kernel,
        name="partial_sums",
        out_shape=(
            jax.ShapeDtypeStruct((2, 16, BLOCK), F32),
            jax.ShapeDtypeStruct((size, LCOLS), BF16),
        ),
        in_specs=[hbm] * 6,
        out_specs=(vmem, hbm),
        scratch_shapes=[
            pltpu.VMEM((size, LCOLS), BF16),
            pltpu.VMEM((size, LCOLS), F32),
            pltpu.VMEM((size, LCOLS), F32),
            pltpu.VMEM((size, LCOLS), F32),
            pltpu.VMEM((size, 2 * LCOLS), BF16),
            pltpu.VMEM((2, STEPS, LCOLS, WIDE), BF16),
            pltpu.VMEM((STEPS, LROWS, WIDE), BF16),
            pltpu.VMEM((STEPS, LCOLS, WIDE), F32),
            pltpu.VMEM((STEPS, LCOLS, WIDE), F32),
            pltpu.VMEM((2 * LCOLS, WIDE), BF16),
            pltpu.VMEM((LROWS, WIDE), F32),
            pltpu.VMEM((STEPS, 4, 24, BLOCK), F32),
            pltpu.VMEM((STEPS, 4, 16, BLOCK), F32),
            pltpu.VMEM((STEPS, 4, 24, BLOCK), F32),
            pltpu.VMEM((3, 4, 4, 24, BLOCK), F32),
            pltpu.VMEM((3, 4, 24, BLOCK), F32),
            pltpu.VMEM((3, 24, BLOCK), F32),
            pltpu.VMEM((4, 3, 4, 16, BLOCK), F32),
            pltpu.VMEM((4, 3, 16, BLOCK), F32),
            pltpu.VMEM((3, 16, BLOCK), F32),
            pltpu.VMEM((STEPS, 3, 24, BLOCK), F32),
            pltpu.VMEM((3, 4, 24, BLOCK), F32),
            pltpu.VMEM((3, 24, BLOCK), F32),
            pltpu.VMEM((128, 8, BLOCK), F32),
            pltpu.VMEM((8, BLOCK), F32),
            pltpu.VMEM((20, 16, BLOCK), F32),
            pltpu.VMEM((5, 2, 16, BLOCK), F32),
            pltpu.VMEM((1, CAP * BLOCK), F32),
            pltpu.VMEM((1, CAP * BLOCK), F32),
            pltpu.SMEM((1, BLOCK), jnp.int32),
            pltpu.VMEM((1, BLOCK), jnp.int32),
            dma((4,)),
            dma, dma, dma((2, STEPS)), dma((STEPS,)),
            dma, dma((4,)), dma, dma((STEPS,)),
            dma((3,)), dma((3,)), dma((3,)),
            dma((3, 4)), dma((3,)), dma((3,)),
            dma((4, 3)), dma((4, 3)), dma((3,)),
            dma((STEPS, 3)), dma((3, 4)), dma((3,)),
            dma, dma((3,)), dma((3,)), dma((3,)), dma,
            dma((20,)), dma((20,)),
        ],
        compiler_params=pltpu.CompilerParams(
            collective_id=0, has_side_effects=True, vmem_limit_bytes=62 << 20
        ),
    )(field, col_profile, row_profile, obs_owned, noise_owned, block_owner.reshape(1, -1))
    moved = pl.pallas_call(
        apply_kernel,
        name="solve_apply",
        out_shape=jax.ShapeDtypeStruct((size, LCOLS), BF16),
        in_specs=[vmem, hbm],
        out_specs=vmem,
        scratch_shapes=[
            pltpu.VMEM((size, LCOLS), F32), pltpu.VMEM((size, LCOLS), BF16), dma
        ],
        compiler_params=pltpu.CompilerParams(vmem_limit_bytes=62 << 20),
    )(sums, field_t)
    return moved.reshape(ensemble.shape)


def solution(mesh):
    in_specs = (
        P(None, "rows", "cols"),
        P("rows", None),
        P("cols", None),
        P(("rows", "cols"), None),
        P(("rows", "cols"), None),
        P(),
    )
    return jax.shard_map(
        on_device, mesh=mesh, in_specs=in_specs, out_specs=P(None, "rows", "cols"),
        check_vma=False,
    )
```

```python
import functools
import math

import jax
import jax.numpy as jnp
from jax import lax
from jax.experimental import pallas as pl
from jax.experimental.pallas import tpu as pltpu
from jax.sharding import PartitionSpec as P

MEMBERS = 64
BLOCK = 128
CAP = 3
LROWS = 48
LCOLS = 128
STEPS = 16
WIDE = 512
AHEAD = 3
LAG2 = 3
LAG3 = 6
ROOT = math.sqrt(MEMBERS - 1)
MESH = pl.DeviceIdType.MESH
F32 = jnp.float32
BF16 = jnp.bfloat16


def here():
    r = lax.axis_index("rows")
    c = lax.axis_index("cols")
    return r // 4, r % 4, c // 2, c % 2


def device(y, x, z, k):
    return (y * 4 + x, z * 2 + k)


def partial_kernel(
    e_hbm, col_hbm, row_hbm, obs_hbm, noise_hbm, owner_hbm,
    sums_ref, et_hbm,
    e_v, ef, esend, erecv, lhs, col_v, row_v, csend, crecv, rhs, rowf, pa, pb, pc,
    ra1, ra2, ra3, rb1, rb2, rb3, rc1, rc2, rc3, slots, pack, got_core, got,
    obs_ref, noise_ref, owner_ref, owner_row, small_sem,
    e_sem, et_sem, col_sem, row_sem,
    es_sem, er_sem, cs_sem, cr_sem,
    sa, sb, sc,
    qa1, qa2, qa3, qb1, qb2, qb3, qc1, qc2, qc3,
    so, qo_z, qo_x, qo_y, qo_k,
    st, qt,
):
    y, x, z, k = here()
    sibling = device(y, x, z, 1 - k)
    turn = 1 - 2 * k

    def zpeer(d):
        return device(y, x, (z + turn * d + 4) % 4, k)

    def xpeer(d):
        return device(y, (x + turn * d + 4) % 4, z, k)

    def ypeer(d):
        return device((y + turn * d + 4) % 4, x, z, k)

    def flat(d):
        return device((y + d // 4) % 4, (x + d % 4) % 4, z, k)

    def remote(src, dst, send, recv, to):
        return pltpu.make_async_remote_copy(
            src_ref=src, dst_ref=dst, send_sem=send, recv_sem=recv,
            device_id=to, device_id_type=MESH,
        )

    def sent(src, sem):
        remote(src, src, sem, sem, sibling).wait_send()

    def landed(dst, sem):
        remote(dst, dst, sem, sem, sibling).wait_recv()

    def span(core, s):
        dz, dx = 3 - s // 4, 3 - s % 4
        way = 1 - 2 * core
        to_z, to_x = (z + way * dz + 4) % 4, (x + way * dx + 4) % 4
        first = ((core * 4 + to_z) * 4 + to_x) * WIDE
        return pl.ds(pl.multiple_of(first, WIDE), WIDE)

    def load_col(which, s):
        core = k if which == 0 else 1 - k
        return pltpu.make_async_copy(
            col_hbm.at[:, span(core, s)], col_v.at[which, s], col_sem.at[which, s]
        )

    def load_row(s):
        return pltpu.make_async_copy(
            row_hbm.at[:, span(k, s)], row_v.at[s], row_sem.at[s]
        )

    load_e = [
        pltpu.make_async_copy(
            e_hbm.at[:, pl.ds(16 * i, 16), :], e_v.at[i], e_sem.at[i]
        )
        for i in range(3)
    ]
    for load in load_e:
        load.start()
    load_small = [
        pltpu.make_async_copy(src, dst, small_sem.at[i])
        for i, (src, dst) in enumerate(
            ((obs_hbm, obs_ref), (noise_hbm, noise_ref), (owner_hbm, owner_ref),
             (owner_hbm, owner_row))
        )
    ]
    for load in load_small:
        load.start()

    barrier = pltpu.get_barrier_semaphore()
    pl.semaphore_signal(barrier, 1, device_id=sibling, device_id_type=MESH)
    for peer in [zpeer(d) for d in (1, 2, 3)] + [flat(d) for d in range(1, 16)]:
        pl.semaphore_signal(barrier, 1, device_id=peer, device_id_type=MESH)

    def start_loads(s, carry):
        load_col(1, s).start()
        load_col(0, s).start()
        load_row(s).start()
        return carry

    lax.fori_loop(0, STEPS, start_loads, 0)

    home = k * 64 + (x * 4 + y) * 4 + z
    pack[...] = jnp.zeros_like(pack)
    for load in load_small:
        load.wait()
    for i in range(CAP):
        pack[i:i + 1, :] = obs_ref[:, i * BLOCK:(i + 1) * BLOCK]
        pack[4 + i:5 + i, :] = noise_ref[:, i * BLOCK:(i + 1) * BLOCK]
    slots[home] = pack[...]

    pl.semaphore_wait(barrier, 19)

    for d in (1, 2, 3):
        remote(slots.at[home], slots.at[home], so, qo_z.at[d - 1], zpeer(d)).start()

    third = MEMBERS * LROWS // 3
    for piece in range(3):
        load_e[piece].wait()
        ef[piece] = e_v[piece].astype(F32).reshape(third, LCOLS)
        for i in range(16):
            at = piece * 16 + i
            plane = ef[piece, pl.ds(i, MEMBERS, stride=16), :]
            esend[at * MEMBERS:(at + 1) * MEMBERS, :] = plane
            lhs[at * MEMBERS:(at + 1) * MEMBERS, 0:LCOLS] = plane.astype(BF16)
        rows = pl.ds(piece * third, third)
        remote(
            esend.at[rows], erecv.at[rows], es_sem, er_sem.at[piece], sibling
        ).start()

    def send_col(s):
        load_col(1, s).wait()
        csend[s] = col_v[1, s].astype(F32)
        remote(csend.at[s], crecv.at[s], cs_sem, cr_sem.at[s], sibling).start()

    for s in range(AHEAD):
        send_col(s)

    for piece in range(3):
        landed(erecv.at[pl.ds(piece * third, third)], er_sem.at[piece])
        lhs[piece * third:(piece + 1) * third, LCOLS:2 * LCOLS] = (
            erecv[piece * third:(piece + 1) * third, :].astype(BF16)
        )
    save_et = pltpu.make_async_copy(lhs.at[:, pl.ds(0, LCOLS)], et_hbm, et_sem)
    save_et.start()

    def compute(s):
        load_col(0, s).wait()
        load_row(s).wait()
        landed(crecv.at[s], cr_sem.at[s])
        rhs[0:LCOLS, :] = col_v[0, s]
        rhs[LCOLS:2 * LCOLS, :] = crecv[s].astype(BF16)
        rowf[...] = row_v[s].astype(F32)
        total = jnp.zeros((MEMBERS, WIDE), F32)
        group = 4
        for g in range(LROWS // group):
            rows = group * MEMBERS
            along = jnp.dot(
                lhs[g * rows:(g + 1) * rows, :], rhs[...], preferred_element_type=F32
            )
            for i in range(group):
                at = g * group + i
                total += along[i * MEMBERS:(i + 1) * MEMBERS] * rowf[at:at + 1, :]
        for q in range(4):
            lanes = slice(q * BLOCK, (q + 1) * BLOCK)
            place = (turn * (q - y) + 4) % 4
            pa[s, place] = total[0:24, lanes]
            pb[s, place] = total[24:40, lanes]
            pc[s, place] = total[40:64, lanes]

    def first_sends(w, j):
        s, dz, dx = 4 * w + j, 3 - w, 3 - j

        @pl.when(dz != 0)
        def _():
            remote(
                pa.at[s], ra1.at[dz - 1, j],
                sa.at[0], qa1.at[dz - 1, j], zpeer(dz),
            ).start()

        if dx != 0:
            remote(
                pb.at[s], rb1.at[w, dx - 1],
                sb.at[0], qb1.at[w, dx - 1], xpeer(dx),
            ).start()

        for d in (1, 2, 3):
            remote(
                pc.at[s, d], rc1.at[s, d - 1],
                sc.at[0], qc1.at[s, d - 1], ypeer(d),
            ).start()

    def second_a(w, j):
        s, dz, dx = 4 * w + j, 3 - w, 3 - j

        @pl.when(dz == 0)
        def _():
            for p in range(3):
                landed(ra1.at[p, j], qa1.at[p, j])
            pa[s] = pa[s] + (
                ra1[0, j] + (ra1[1, j] + ra1[2, j])
            )

            if dx != 0:
                remote(
                    pa.at[s], ra2.at[dx - 1],
                    sa.at[1], qa2.at[dx - 1], xpeer(dx),
                ).start()

    def second_b(w, j):
        s, dz, dx = 4 * w + j, 3 - w, 3 - j

        if dx == 0:
            for p in range(3):
                landed(rb1.at[w, p], qb1.at[w, p])
            pb[s] = pb[s] + (rb1[w, 0] + (rb1[w, 1] + rb1[w, 2]))
            for d in (1, 2, 3):
                remote(
                    pb.at[s, d], rb2.at[w, d - 1],
                    sb.at[1], qb2.at[w, d - 1], ypeer(d),
                ).start()

    def second_c(w, j):
        s, dz, dx = 4 * w + j, 3 - w, 3 - j
        for p in range(3):
            landed(rc1.at[s, p], qc1.at[s, p])
        pc[s, 0] = pc[s, 0] + (rc1[s, 0] + (rc1[s, 1] + rc1[s, 2]))

        @pl.when(dz != 0)
        def _():
            remote(
                pc.at[s, 0], rc2.at[dz - 1, j],
                sc.at[1], qc2.at[dz - 1, j], zpeer(dz),
            ).start()

    def third_a():
        s = STEPS - 1
        for p in range(3):
            landed(ra2.at[p], qa2.at[p])
        pa[s] = pa[s] + (ra2[0] + (ra2[1] + ra2[2]))
        for d in (1, 2, 3):
            remote(
                pa.at[s, d], ra3.at[d - 1],
                sa.at[2], qa3.at[d - 1], ypeer(d),
            ).start()

    def third_b(w, j):
        s, dz, dx = 4 * w + j, 3 - w, 3 - j

        if dx == 0:
            for p in range(3):
                landed(rb2.at[w, p], qb2.at[w, p])
            pb[s, 0] = pb[s, 0] + (rb2[w, 0] + (rb2[w, 1] + rb2[w, 2]))

            @pl.when(dz != 0)
            def _():
                remote(
                    pb.at[s, 0], rb3.at[dz - 1],
                    sb.at[2], qb3.at[dz - 1], zpeer(dz),
                ).start()

    def third_c(w, j):
        s, dz, dx = 4 * w + j, 3 - w, 3 - j

        @pl.when(dz == 0)
        def _():
            for p in range(3):
                landed(rc2.at[p, j], qc2.at[p, j])
            pc[s, 0] = pc[s, 0] + (
                rc2[0, j] + (rc2[1, j] + rc2[2, j])
            )

            if dx != 0:
                remote(
                    pc.at[s, 0], rc3.at[dx - 1],
                    sc.at[2], qc3.at[dx - 1], xpeer(dx),
                ).start()

    base_y = k * 64 + (x * 4 + y) * 4
    base_x = k * 64 + x * 16
    base_k = k * 64

    def slots_y():
        for d in (1, 2, 3):
            landed(slots.at[home], qo_z.at[d - 1])
        mine = slots.at[pl.ds(base_y, 4)]
        for d in (1, 2, 3):
            remote(mine, mine, so, qo_y.at[d - 1], ypeer(d)).start()

    def slots_x():
        for d in (1, 2, 3):
            landed(slots.at[pl.ds(base_y, 4)], qo_y.at[d - 1])
        mine = slots.at[pl.ds(base_x, 16)]
        for d in (1, 2, 3):
            remote(mine, mine, so, qo_x.at[d - 1], xpeer(d)).start()

    def slots_k():
        for d in (1, 2, 3):
            landed(slots.at[pl.ds(base_x, 16)], qo_x.at[d - 1])
        mine = slots.at[pl.ds(base_k, 64)]
        remote(mine, mine, so, qo_k, sibling).start()

    def lagged(events, w, j, lag):
        back = (j - lag) // 4
        late, at = w + back, (j - lag) % 4

        def run():
            for event in events:
                event(late, at)

        if back == 0:
            run()
        else:
            pl.when(late >= 0)(run)

    def phase(w, carry):
        for j in range(4):
            s = 4 * w + j
            pl.when(s + AHEAD < STEPS)(functools.partial(send_col, s + AHEAD))
            compute(s)
            first_sends(w, j)
            second_a(w, j)
            lagged((second_b,), w, j, 2)
            lagged((second_c, third_c), w, j, 3)
            lagged((third_b,), w, j, 5)
        pl.when(w == 0)(slots_x)
        pl.when(w == 1)(slots_k)
        return carry

    slots_y()
    lax.fori_loop(0, STEPS // 4, phase, 0)

    last = STEPS - 1
    second_c(3, 1)
    third_c(3, 1)
    third_b(2, 3)
    second_b(3, 3)
    third_a()
    second_c(3, 2)
    third_c(3, 2)
    second_c(3, 3)
    third_c(3, 3)
    third_b(3, 3)

    landed(slots.at[pl.ds(base_k, 64)], qo_k)
    me = ((k * 4 + z) * 4 + x) * 4 + y
    owner = owner_ref[0, me]
    owners = owner_row[...]
    block_at = lax.broadcasted_iota(jnp.int32, (1, BLOCK), 1)
    before = jnp.logical_and(owners == owner, block_at < me)
    rank = jnp.sum(jnp.where(before, 1.0, 0.0), axis=1, keepdims=True)
    o_row, o_col = owner // 8, owner % 8
    found = slots[
        (o_col % 2) * 64 + (o_row % 4) * 16 + (o_row // 4) * 4 + o_col // 2
    ]
    observed = jnp.where(
        rank < 0.5, found[0:1], jnp.where(rank < 1.5, found[1:2], found[2:3])
    )
    variance = jnp.where(
        rank < 0.5, found[4:5], jnp.where(rank < 1.5, found[5:6], found[6:7])
    )
    weight = 1.0 / variance

    for d in range(3):
        landed(ra3.at[d], qa3.at[d])
        landed(rb3.at[d], qb3.at[d])
        landed(rc3.at[d], qc3.at[d])
    predictions = jnp.concatenate(
        [
            pa[last, 0] + (ra3[0] + (ra3[1] + ra3[2])),
            pb[last, 0] + (rb3[0] + (rb3[1] + rb3[2])),
            pc[last, 0] + (rc3[0] + (rc3[1] + rc3[2])),
        ],
        axis=0,
    )
    mean = jnp.mean(predictions, axis=0, keepdims=True)
    anomalies = (predictions - mean) * (1.0 / ROOT)
    scaled = anomalies * weight
    target = anomalies + (observed - mean)
    blank = jnp.zeros((MEMBERS, BLOCK), F32)
    contract = (((1,), (1,)), ((), ()))
    left = jnp.concatenate([scaled[0:16], scaled[32:48]], axis=0)
    right = jnp.concatenate([scaled[16:32], scaled[48:64]], axis=0)
    packed = lax.dot_general(
        left, jnp.concatenate([target, blank], axis=0), contract,
        precision=lax.Precision.HIGHEST, preferred_element_type=F32,
    ) + lax.dot_general(
        right, jnp.concatenate([blank, target], axis=0), contract,
        precision=lax.Precision.HIGHEST, preferred_element_type=F32,
    )
    got[0, 0] = packed[0:16]
    got[0, 1] = packed[16:32]

    remote(got.at[0, 1 - k], got_core.at[0], st.at[0], qt.at[0], sibling).start()
    landed(got_core.at[0], qt.at[0])
    got[1, 0] = got[0, k] + got_core[0]
    for d in (1, 2, 3):
        remote(
            got.at[1, 0], got_core.at[d], st.at[d], qt.at[d], zpeer(d)
        ).start()
    for d in (1, 2, 3):
        landed(got_core.at[d], qt.at[d])
    got[2, 0] = got[1, 0] + (got_core[1] + (got_core[2] + got_core[3]))
    for d in range(1, 16):
        remote(
            got.at[2, 0], got_core.at[3 + d], st.at[3 + d], qt.at[3 + d], flat(d)
        ).start()
    total = got[2, 0]
    for d in range(1, 16):
        landed(got_core.at[3 + d], qt.at[3 + d])
        total += got_core[3 + d]
    got[3, 0] = total
    end = 19
    whole = 3
    remote(got.at[whole, 0], got_core.at[end], st.at[end], qt.at[end], sibling).start()
    sums_ref[k] = got[whole, 0]
    landed(got_core.at[end], qt.at[end])
    sums_ref[1 - k] = got_core[end]

    save_et.wait()
    sent(esend, es_sem)
    sent(csend, cs_sem)
    sent(pa.at[pl.ds(0, 12), :], sa.at[0])
    sent(pa.at[pl.ds(0, 3), :], sa.at[1])
    sent(pa.at[0, pl.ds(0, 3)], sa.at[2])
    sent(pb.at[pl.ds(0, 12), :], sb.at[0])
    sent(pb.at[pl.ds(0, 4), pl.ds(0, 3)], sb.at[1])
    sent(pb.at[0, pl.ds(0, 3)], sb.at[2])
    sent(pc.at[pl.ds(0, 16), pl.ds(0, 3)], sc.at[0])
    sent(pc.at[pl.ds(0, 12), 0], sc.at[1])
    sent(pc.at[0, pl.ds(0, 3)], sc.at[2])
    sent(slots.at[pl.ds(0, 3 + 12 + 48 + 64)], so)
    for i in range(20):
        sent(got_core.at[0], st.at[i])


def lane(panel, at):
    return jnp.broadcast_to(panel[:, at:at + 1], panel.shape)


def sub(panel, at):
    return jnp.broadcast_to(panel[at:at + 1], panel.shape)


def pivot_four(panel, column, t):
    at = lax.broadcasted_iota(jnp.int32, panel.shape, 0)
    c = [lane(panel, column + t + i) for i in range(4)]
    r = [sub(panel, t + i) for i in range(4)]
    a, q, d = sub(c[0], t), sub(c[0], t + 1), sub(c[1], t + 1)
    e00, e01, e10, e11 = (
        sub(c[0], t + 2), sub(c[1], t + 2), sub(c[0], t + 3), sub(c[1], t + 3)
    )
    f, g, h = sub(c[2], t + 2), sub(c[2], t + 3), sub(c[3], t + 3)
    inv = 1.0 / (a * d - q * q)
    w00, w01 = (e00 * d - e01 * q) * inv, (e01 * a - e00 * q) * inv
    w10, w11 = (e10 * d - e11 * q) * inv, (e11 * a - e10 * q) * inv
    f = f - (w00 * e00 + w01 * e01)
    g = g - (w00 * e10 + w01 * e11)
    h = h - (w10 * e10 + w11 * e11)
    rest = 1.0 / (f * h - g * g)
    u = r[2] - (w00 * r[0] + w01 * r[1])
    v = r[3] - (w10 * r[0] + w11 * r[1])
    n2, n3 = (h * u - g * v) * rest, (f * v - g * u) * rest
    n0 = (d * r[0] - q * r[1]) * inv - (w00 * n2 + w10 * n3)
    n1 = (a * r[1] - q * r[0]) * inv - (w01 * n2 + w11 * n3)
    new = panel - ((c[0] * n0 + c[1] * n1) + (c[2] * n2 + c[3] * n3))
    for i, row in enumerate((n0, n1, n2, n3)):
        new = jnp.where(at == t + i, row, new)
    return new


def eliminate(grid):
    panels = [grid[8 * i:8 * i + 8] for i in range(8)]
    for b in range(8):
        columns = [
            [lane(panels[i], 8 * b + t) for t in range(8)] if i != b else None
            for i in range(8)
        ]
        done = pivot_four(pivot_four(panels[b], 8 * b, 0), 8 * b, 4)
        rows = [sub(done, t) for t in range(8)]
        for i in range(8):
            if i != b:
                m = [columns[i][t] * rows[t] for t in range(8)]
                panels[i] = panels[i] - (
                    ((m[0] + m[1]) + (m[2] + m[3])) + ((m[4] + m[5]) + (m[6] + m[7]))
                )
        panels[b] = done
    return jnp.concatenate(panels, axis=0)


def apply_kernel(sums_ref, et_hbm, out_ref, full, et_ref, et_sem):
    load = pltpu.make_async_copy(et_hbm, et_ref, et_sem)
    load.start()
    low, high = sums_ref[0], sums_ref[1]
    both = jnp.concatenate(
        [low, pltpu.roll(low, 64, 1), high, pltpu.roll(high, 64, 1)], axis=0
    )
    row_at = lax.broadcasted_iota(jnp.int32, (MEMBERS, 2 * MEMBERS), 0)
    lane_at = lax.broadcasted_iota(jnp.int32, (MEMBERS, 2 * MEMBERS), 1)
    left = lane_at < MEMBERS
    r_col = jnp.sum(jnp.where(left, both, 0.0), axis=1, keepdims=True) * (1.0 / MEMBERS)
    eye = jnp.where(row_at == lane_at, 1.0, 0.0)
    grid = eliminate(
        jnp.where(
            left, (both - r_col) + eye, jnp.where(lane_at - MEMBERS == row_at, 1.0, 0.0)
        )
    )
    inverse = jnp.where(left, pltpu.roll(grid, 64, 1), 0.0)
    shift = jnp.sum(inverse * r_col, axis=0, keepdims=True)
    gain_t = jnp.where(left, shift - ROOT * (eye - inverse), 0.0)
    centre = jnp.sum(gain_t, axis=1, keepdims=True) * (1.0 / MEMBERS)
    moves = jnp.where(left, (gain_t - centre) * (1.0 / ROOT), 0.0)
    one = moves.astype(BF16).astype(F32)
    two = (moves - one).astype(BF16).astype(F32)
    three = moves - one - two
    factors = jnp.concatenate(
        [(one + pltpu.roll(two, 64, 1)).astype(BF16), three.astype(BF16)], axis=1
    )
    zero = jnp.zeros((MEMBERS, 2 * BLOCK), BF16)
    load.wait()
    for g in range(LROWS // 2):
        at = 2 * g * MEMBERS
        pair = jnp.concatenate(
            [et_ref[at:at + MEMBERS, :], et_ref[at + MEMBERS:at + 2 * MEMBERS, :]], axis=1
        )
        moved = pair.astype(F32) + jnp.dot(
            factors, jnp.concatenate([pair, pair, pair, zero], axis=0),
            preferred_element_type=F32,
        )
        full[pl.ds(2 * g, MEMBERS, stride=LROWS), :] = moved[:, 0:BLOCK]
        full[pl.ds(2 * g + 1, MEMBERS, stride=LROWS), :] = moved[:, BLOCK:2 * BLOCK]
    out_ref[...] = full[...].astype(BF16)


def on_device(ensemble, row_profile, col_profile, obs_owned, noise_owned, block_owner):
    hbm = pl.BlockSpec(memory_space=pltpu.HBM)
    vmem = pl.BlockSpec(memory_space=pltpu.VMEM)
    dma = pltpu.SemaphoreType.DMA
    size = MEMBERS * LROWS
    sums, field_t = pl.pallas_call(
        partial_kernel,
        name="partial_sums",
        out_shape=(
            jax.ShapeDtypeStruct((2, 16, BLOCK), F32),
            jax.ShapeDtypeStruct((size, LCOLS), BF16),
        ),
        in_specs=[hbm] * 6,
        out_specs=(vmem, hbm),
        scratch_shapes=[
            pltpu.VMEM((3, MEMBERS, 16, LCOLS), BF16),
            pltpu.VMEM((3, size // 3, LCOLS), F32),
            pltpu.VMEM((size, LCOLS), F32),
            pltpu.VMEM((size, LCOLS), F32),
            pltpu.VMEM((size, 2 * LCOLS), BF16),
            pltpu.VMEM((2, STEPS, LCOLS, WIDE), BF16),
            pltpu.VMEM((STEPS, LROWS, WIDE), BF16),
            pltpu.VMEM((STEPS, LCOLS, WIDE), F32),
            pltpu.VMEM((STEPS, LCOLS, WIDE), F32),
            pltpu.VMEM((2 * LCOLS, WIDE), BF16),
            pltpu.VMEM((LROWS, WIDE), F32),
            pltpu.VMEM((STEPS, 4, 24, BLOCK), F32),
            pltpu.VMEM((STEPS, 4, 16, BLOCK), F32),
            pltpu.VMEM((STEPS, 4, 24, BLOCK), F32),
            pltpu.VMEM((3, 4, 4, 24, BLOCK), F32),
            pltpu.VMEM((3, 4, 24, BLOCK), F32),
            pltpu.VMEM((3, 24, BLOCK), F32),
            pltpu.VMEM((4, 3, 4, 16, BLOCK), F32),
            pltpu.VMEM((4, 3, 16, BLOCK), F32),
            pltpu.VMEM((3, 16, BLOCK), F32),
            pltpu.VMEM((STEPS, 3, 24, BLOCK), F32),
            pltpu.VMEM((3, 4, 24, BLOCK), F32),
            pltpu.VMEM((3, 24, BLOCK), F32),
            pltpu.VMEM((128, 8, BLOCK), F32),
            pltpu.VMEM((8, BLOCK), F32),
            pltpu.VMEM((20, 16, BLOCK), F32),
            pltpu.VMEM((5, 2, 16, BLOCK), F32),
            pltpu.VMEM((1, CAP * BLOCK), F32),
            pltpu.VMEM((1, CAP * BLOCK), F32),
            pltpu.SMEM((1, BLOCK), jnp.int32),
            pltpu.VMEM((1, BLOCK), jnp.int32),
            dma((4,)),
            dma((3,)), dma, dma((2, STEPS)), dma((STEPS,)),
            dma, dma((3,)), dma, dma((STEPS,)),
            dma((3,)), dma((3,)), dma((3,)),
            dma((3, 4)), dma((3,)), dma((3,)),
            dma((4, 3)), dma((4, 3)), dma((3,)),
            dma((STEPS, 3)), dma((3, 4)), dma((3,)),
            dma, dma((3,)), dma((3,)), dma((3,)), dma,
            dma((20,)), dma((20,)),
        ],
        compiler_params=pltpu.CompilerParams(
            collective_id=0, has_side_effects=True, vmem_limit_bytes=62 << 20
        ),
    )(ensemble, col_profile, row_profile, obs_owned, noise_owned, block_owner.reshape(1, -1))
    moved = pl.pallas_call(
        apply_kernel,
        name="solve_apply",
        out_shape=jax.ShapeDtypeStruct((size, LCOLS), BF16),
        in_specs=[vmem, hbm],
        out_specs=vmem,
        scratch_shapes=[
            pltpu.VMEM((size, LCOLS), F32), pltpu.VMEM((size, LCOLS), BF16), dma
        ],
        compiler_params=pltpu.CompilerParams(vmem_limit_bytes=62 << 20),
    )(sums, field_t)
    return moved.reshape(ensemble.shape)


def solution(mesh):
    in_specs = (
        P(None, "rows", "cols"),
        P("rows", None),
        P("cols", None),
        P(("rows", "cols"), None),
        P(("rows", "cols"), None),
        P(),
    )
    return jax.shard_map(
        on_device, mesh=mesh, in_specs=in_specs, out_specs=P(None, "rows", "cols"),
        check_vma=False,
    )
```

```python
import functools
import math

import jax
import jax.numpy as jnp
from jax import lax
from jax.experimental import pallas as pl
from jax.experimental.pallas import tpu as pltpu
from jax.sharding import PartitionSpec as P

MEMBERS = 64
BLOCK = 128
CAP = 3
LROWS = 48
LCOLS = 128
STEPS = 16
WIDE = 512
AHEAD = 3
LAG2 = 3
LAG3 = 6
ROOT = math.sqrt(MEMBERS - 1)
MESH = pl.DeviceIdType.MESH
F32 = jnp.float32
BF16 = jnp.bfloat16


def here():
    r = lax.axis_index("rows")
    c = lax.axis_index("cols")
    return r // 4, r % 4, c // 2, c % 2


def device(y, x, z, k):
    return (y * 4 + x, z * 2 + k)


def partial_kernel(
    e_hbm, col_hbm, row_hbm, obs_hbm, noise_hbm, owner_hbm,
    sums_ref, et_hbm,
    e_v, ef, esend, erecv, lhs, col_v, row_v, csend, crecv, rhs, rowf, pa, pb, pc,
    ra1, ra2, ra3, rb1, rb2, rb3, rc1, rc2, rc3, slots, pack, got_core, got,
    obs_ref, noise_ref, owner_ref, owner_row, small_sem,
    e_sem, et_sem, col_sem, row_sem,
    es_sem, er_sem, cs_sem, cr_sem,
    sa, sb, sc,
    qa1, qa2, qa3, qb1, qb2, qb3, qc1, qc2, qc3,
    so, qo_z, qo_x, qo_y, qo_k,
    st, qt,
):
    y, x, z, k = here()
    sibling = device(y, x, z, 1 - k)
    turn = 1 - 2 * k

    def zpeer(d):
        return device(y, x, (z + turn * d + 4) % 4, k)

    def xpeer(d):
        return device(y, (x + turn * d + 4) % 4, z, k)

    def ypeer(d):
        return device((y + turn * d + 4) % 4, x, z, k)

    def flat(d):
        return device((y + d // 4) % 4, (x + d % 4) % 4, z, k)

    def remote(src, dst, send, recv, to):
        return pltpu.make_async_remote_copy(
            src_ref=src, dst_ref=dst, send_sem=send, recv_sem=recv,
            device_id=to, device_id_type=MESH,
        )

    def sent(src, sem):
        remote(src, src, sem, sem, sibling).wait_send()

    def landed(dst, sem):
        remote(dst, dst, sem, sem, sibling).wait_recv()

    def span(core, s):
        dz, dx = 3 - s // 4, 3 - s % 4
        way = 1 - 2 * core
        to_z, to_x = (z + way * dz + 4) % 4, (x + way * dx + 4) % 4
        first = ((core * 4 + to_z) * 4 + to_x) * WIDE
        return pl.ds(pl.multiple_of(first, WIDE), WIDE)

    def load_col(which, s):
        core = k if which == 0 else 1 - k
        return pltpu.make_async_copy(
            col_hbm.at[:, span(core, s)], col_v.at[which, s], col_sem.at[which, s]
        )

    def load_row(s):
        return pltpu.make_async_copy(
            row_hbm.at[:, span(k, s)], row_v.at[s], row_sem.at[s]
        )

    load_e = [
        pltpu.make_async_copy(
            e_hbm.at[:, pl.ds(16 * i, 16), :], e_v.at[i], e_sem.at[i]
        )
        for i in range(3)
    ]
    for load in load_e:
        load.start()
    load_small = [
        pltpu.make_async_copy(src, dst, small_sem.at[i])
        for i, (src, dst) in enumerate(
            ((obs_hbm, obs_ref), (noise_hbm, noise_ref), (owner_hbm, owner_ref),
             (owner_hbm, owner_row))
        )
    ]
    for load in load_small:
        load.start()

    barrier = pltpu.get_barrier_semaphore()
    pl.semaphore_signal(barrier, 1, device_id=sibling, device_id_type=MESH)
    for peer in [zpeer(d) for d in (1, 2, 3)] + [flat(d) for d in range(1, 16)]:
        pl.semaphore_signal(barrier, 1, device_id=peer, device_id_type=MESH)

    def start_loads(s, carry):
        load_col(1, s).start()
        load_col(0, s).start()
        load_row(s).start()
        return carry

    lax.fori_loop(0, STEPS, start_loads, 0)

    home = k * 64 + (x * 4 + y) * 4 + z
    pack[...] = jnp.zeros_like(pack)
    for load in load_small:
        load.wait()
    for i in range(CAP):
        pack[i:i + 1, :] = obs_ref[:, i * BLOCK:(i + 1) * BLOCK]
        pack[4 + i:5 + i, :] = noise_ref[:, i * BLOCK:(i + 1) * BLOCK]
    slots[home] = pack[...]

    pl.semaphore_wait(barrier, 19)

    for d in (1, 2, 3):
        remote(slots.at[home], slots.at[home], so, qo_z.at[d - 1], zpeer(d)).start()

    third = MEMBERS * LROWS // 3
    for piece in range(3):
        load_e[piece].wait()
        ef[piece] = e_v[piece].astype(F32).reshape(third, LCOLS)
        for i in range(16):
            at = piece * 16 + i
            plane = ef[piece, pl.ds(i, MEMBERS, stride=16), :]
            esend[at * MEMBERS:(at + 1) * MEMBERS, :] = plane
            lhs[at * MEMBERS:(at + 1) * MEMBERS, 0:LCOLS] = plane.astype(BF16)
        rows = pl.ds(piece * third, third)
        remote(
            esend.at[rows], erecv.at[rows], es_sem, er_sem.at[piece], sibling
        ).start()

    def send_col(s):
        load_col(1, s).wait()
        csend[s] = col_v[1, s].astype(F32)
        remote(csend.at[s], crecv.at[s], cs_sem, cr_sem.at[s], sibling).start()

    for s in range(AHEAD):
        send_col(s)

    for piece in range(3):
        landed(erecv.at[pl.ds(piece * third, third)], er_sem.at[piece])
        lhs[piece * third:(piece + 1) * third, LCOLS:2 * LCOLS] = (
            erecv[piece * third:(piece + 1) * third, :].astype(BF16)
        )
    save_et = pltpu.make_async_copy(lhs.at[:, pl.ds(0, LCOLS)], et_hbm, et_sem)
    save_et.start()

    def compute(s):
        load_col(0, s).wait()
        load_row(s).wait()
        landed(crecv.at[s], cr_sem.at[s])
        rhs[0:LCOLS, :] = col_v[0, s]
        rhs[LCOLS:2 * LCOLS, :] = crecv[s].astype(BF16)
        rowf[...] = row_v[s].astype(F32)
        total = jnp.zeros((MEMBERS, WIDE), F32)
        group = 4
        for g in range(LROWS // group):
            rows = group * MEMBERS
            along = jnp.dot(
                lhs[g * rows:(g + 1) * rows, :], rhs[...], preferred_element_type=F32
            )
            for i in range(group):
                at = g * group + i
                total += along[i * MEMBERS:(i + 1) * MEMBERS] * rowf[at:at + 1, :]
        for q in range(4):
            lanes = slice(q * BLOCK, (q + 1) * BLOCK)
            place = (turn * (q - y) + 4) % 4
            pa[s, place] = total[0:24, lanes]
            pb[s, place] = total[24:40, lanes]
            pc[s, place] = total[40:64, lanes]

    def first_sends(w, j):
        s, dz, dx = 4 * w + j, 3 - w, 3 - j

        @pl.when(dz != 0)
        def _():
            remote(
                pa.at[s], ra1.at[dz - 1, j],
                sa.at[0], qa1.at[dz - 1, j], zpeer(dz),
            ).start()

        if dx != 0:
            remote(
                pb.at[s], rb1.at[w, dx - 1],
                sb.at[0], qb1.at[w, dx - 1], xpeer(dx),
            ).start()

        for d in (2, 1, 3):
            remote(
                pc.at[s, d], rc1.at[s, d - 1],
                sc.at[0], qc1.at[s, d - 1], ypeer(d),
            ).start()

    def second_a(w, j):
        s, dz, dx = 4 * w + j, 3 - w, 3 - j

        @pl.when(dz == 0)
        def _():
            for p in range(3):
                landed(ra1.at[p, j], qa1.at[p, j])
            pa[s] = pa[s] + (
                ra1[0, j] + (ra1[1, j] + ra1[2, j])
            )

            if dx != 0:
                remote(
                    pa.at[s], ra2.at[dx - 1],
                    sa.at[1], qa2.at[dx - 1], xpeer(dx),
                ).start()

    def second_b(w, j):
        s, dz, dx = 4 * w + j, 3 - w, 3 - j

        if dx == 0:
            for p in range(3):
                landed(rb1.at[w, p], qb1.at[w, p])
            pb[s] = pb[s] + (rb1[w, 0] + (rb1[w, 1] + rb1[w, 2]))
            for d in (2, 1, 3):
                remote(
                    pb.at[s, d], rb2.at[w, d - 1],
                    sb.at[1], qb2.at[w, d - 1], ypeer(d),
                ).start()

    def second_c(w, j):
        s, dz, dx = 4 * w + j, 3 - w, 3 - j
        for p in range(3):
            landed(rc1.at[s, p], qc1.at[s, p])
        pc[s, 0] = pc[s, 0] + (rc1[s, 0] + (rc1[s, 1] + rc1[s, 2]))

        @pl.when(dz != 0)
        def _():
            remote(
                pc.at[s, 0], rc2.at[dz - 1, j],
                sc.at[1], qc2.at[dz - 1, j], zpeer(dz),
            ).start()

    def third_a():
        s = STEPS - 1
        for p in range(3):
            landed(ra2.at[p], qa2.at[p])
        pa[s] = pa[s] + (ra2[0] + (ra2[1] + ra2[2]))
        for d in (2, 1, 3):
            remote(
                pa.at[s, d], ra3.at[d - 1],
                sa.at[2], qa3.at[d - 1], ypeer(d),
            ).start()

    def third_b(w, j):
        s, dz, dx = 4 * w + j, 3 - w, 3 - j

        if dx == 0:
            for p in range(3):
                landed(rb2.at[w, p], qb2.at[w, p])
            pb[s, 0] = pb[s, 0] + (rb2[w, 0] + (rb2[w, 1] + rb2[w, 2]))

            @pl.when(dz != 0)
            def _():
                remote(
                    pb.at[s, 0], rb3.at[dz - 1],
                    sb.at[2], qb3.at[dz - 1], zpeer(dz),
                ).start()

    def third_c(w, j):
        s, dz, dx = 4 * w + j, 3 - w, 3 - j

        @pl.when(dz == 0)
        def _():
            for p in range(3):
                landed(rc2.at[p, j], qc2.at[p, j])
            pc[s, 0] = pc[s, 0] + (
                rc2[0, j] + (rc2[1, j] + rc2[2, j])
            )

            if dx != 0:
                remote(
                    pc.at[s, 0], rc3.at[dx - 1],
                    sc.at[2], qc3.at[dx - 1], xpeer(dx),
                ).start()

    base_y = k * 64 + (x * 4 + y) * 4
    base_x = k * 64 + x * 16
    base_k = k * 64

    def slots_y():
        for d in (1, 2, 3):
            landed(slots.at[home], qo_z.at[d - 1])
        mine = slots.at[pl.ds(base_y, 4)]
        for d in (1, 2, 3):
            remote(mine, mine, so, qo_y.at[d - 1], ypeer(d)).start()

    def slots_x():
        for d in (1, 2, 3):
            landed(slots.at[pl.ds(base_y, 4)], qo_y.at[d - 1])
        mine = slots.at[pl.ds(base_x, 16)]
        for d in (1, 2, 3):
            remote(mine, mine, so, qo_x.at[d - 1], xpeer(d)).start()

    def slots_k():
        for d in (1, 2, 3):
            landed(slots.at[pl.ds(base_x, 16)], qo_x.at[d - 1])
        mine = slots.at[pl.ds(base_k, 64)]
        remote(mine, mine, so, qo_k, sibling).start()

    def lagged(events, w, j, lag):
        back = (j - lag) // 4
        late, at = w + back, (j - lag) % 4

        def run():
            for event in events:
                event(late, at)

        if back == 0:
            run()
        else:
            pl.when(late >= 0)(run)

    def phase(w, carry):
        for j in range(4):
            s = 4 * w + j
            pl.when(s + AHEAD < STEPS)(functools.partial(send_col, s + AHEAD))
            compute(s)
            first_sends(w, j)
            second_a(w, j)
            lagged((second_b,), w, j, 2)
            lagged((second_c, third_c), w, j, 3)
            lagged((third_b,), w, j, 5)
        pl.when(w == 0)(slots_x)
        pl.when(w == 1)(slots_k)
        return carry

    slots_y()
    lax.fori_loop(0, STEPS // 4, phase, 0)

    last = STEPS - 1
    second_c(3, 1)
    third_c(3, 1)
    third_b(2, 3)
    second_b(3, 3)
    third_a()
    second_c(3, 2)
    third_c(3, 2)
    second_c(3, 3)
    third_c(3, 3)
    third_b(3, 3)

    landed(slots.at[pl.ds(base_k, 64)], qo_k)
    me = ((k * 4 + z) * 4 + x) * 4 + y
    owner = owner_ref[0, me]
    owners = owner_row[...]
    block_at = lax.broadcasted_iota(jnp.int32, (1, BLOCK), 1)
    before = jnp.logical_and(owners == owner, block_at < me)
    rank = jnp.sum(jnp.where(before, 1.0, 0.0), axis=1, keepdims=True)
    o_row, o_col = owner // 8, owner % 8
    found = slots[
        (o_col % 2) * 64 + (o_row % 4) * 16 + (o_row // 4) * 4 + o_col // 2
    ]
    observed = jnp.where(
        rank < 0.5, found[0:1], jnp.where(rank < 1.5, found[1:2], found[2:3])
    )
    variance = jnp.where(
        rank < 0.5, found[4:5], jnp.where(rank < 1.5, found[5:6], found[6:7])
    )
    weight = 1.0 / variance

    for d in range(3):
        landed(ra3.at[d], qa3.at[d])
        landed(rb3.at[d], qb3.at[d])
        landed(rc3.at[d], qc3.at[d])
    predictions = jnp.concatenate(
        [
            pa[last, 0] + (ra3[0] + (ra3[1] + ra3[2])),
            pb[last, 0] + (rb3[0] + (rb3[1] + rb3[2])),
            pc[last, 0] + (rc3[0] + (rc3[1] + rc3[2])),
        ],
        axis=0,
    )
    mean = jnp.mean(predictions, axis=0, keepdims=True)
    anomalies = (predictions - mean) * (1.0 / ROOT)
    scaled = anomalies * weight
    target = anomalies + (observed - mean)
    blank = jnp.zeros((MEMBERS, BLOCK), F32)
    contract = (((1,), (1,)), ((), ()))
    left = jnp.concatenate([scaled[0:16], scaled[32:48]], axis=0)
    right = jnp.concatenate([scaled[16:32], scaled[48:64]], axis=0)
    packed = lax.dot_general(
        left, jnp.concatenate([target, blank], axis=0), contract,
        precision=lax.Precision.HIGHEST, preferred_element_type=F32,
    ) + lax.dot_general(
        right, jnp.concatenate([blank, target], axis=0), contract,
        precision=lax.Precision.HIGHEST, preferred_element_type=F32,
    )
    got[0, 0] = packed[0:16]
    got[0, 1] = packed[16:32]

    remote(got.at[0, 1 - k], got_core.at[0], st.at[0], qt.at[0], sibling).start()
    landed(got_core.at[0], qt.at[0])
    got[1, 0] = got[0, k] + got_core[0]
    for d in (2, 1, 3):
        remote(
            got.at[1, 0], got_core.at[d], st.at[d], qt.at[d], zpeer(d)
        ).start()
    for d in (1, 2, 3):
        landed(got_core.at[d], qt.at[d])
    got[2, 0] = got[1, 0] + (got_core[1] + (got_core[2] + got_core[3]))
    for d in (10, 9, 11, 6, 14, 5, 7, 13, 15, 8, 2, 4, 12, 1, 3):
        remote(
            got.at[2, 0], got_core.at[3 + d], st.at[3 + d], qt.at[3 + d], flat(d)
        ).start()
    total = got[2, 0]
    for d in range(1, 16):
        landed(got_core.at[3 + d], qt.at[3 + d])
        total += got_core[3 + d]
    got[3, 0] = total
    end = 19
    whole = 3
    remote(got.at[whole, 0], got_core.at[end], st.at[end], qt.at[end], sibling).start()
    sums_ref[k] = got[whole, 0]
    landed(got_core.at[end], qt.at[end])
    sums_ref[1 - k] = got_core[end]

    save_et.wait()
    sent(esend, es_sem)
    sent(csend, cs_sem)
    sent(pa.at[pl.ds(0, 12), :], sa.at[0])
    sent(pa.at[pl.ds(0, 3), :], sa.at[1])
    sent(pa.at[0, pl.ds(0, 3)], sa.at[2])
    sent(pb.at[pl.ds(0, 12), :], sb.at[0])
    sent(pb.at[pl.ds(0, 4), pl.ds(0, 3)], sb.at[1])
    sent(pb.at[0, pl.ds(0, 3)], sb.at[2])
    sent(pc.at[pl.ds(0, 16), pl.ds(0, 3)], sc.at[0])
    sent(pc.at[pl.ds(0, 12), 0], sc.at[1])
    sent(pc.at[0, pl.ds(0, 3)], sc.at[2])
    sent(slots.at[pl.ds(0, 3 + 12 + 48 + 64)], so)
    for i in range(20):
        sent(got_core.at[0], st.at[i])


def lane(panel, at):
    return jnp.broadcast_to(panel[:, at:at + 1], panel.shape)


def sub(panel, at):
    return jnp.broadcast_to(panel[at:at + 1], panel.shape)


def pivot_four(panel, column, t):
    at = lax.broadcasted_iota(jnp.int32, panel.shape, 0)
    c = [lane(panel, column + t + i) for i in range(4)]
    r = [sub(panel, t + i) for i in range(4)]
    a, q, d = sub(c[0], t), sub(c[0], t + 1), sub(c[1], t + 1)
    e00, e01, e10, e11 = (
        sub(c[0], t + 2), sub(c[1], t + 2), sub(c[0], t + 3), sub(c[1], t + 3)
    )
    f, g, h = sub(c[2], t + 2), sub(c[2], t + 3), sub(c[3], t + 3)
    inv = 1.0 / (a * d - q * q)
    w00, w01 = (e00 * d - e01 * q) * inv, (e01 * a - e00 * q) * inv
    w10, w11 = (e10 * d - e11 * q) * inv, (e11 * a - e10 * q) * inv
    f = f - (w00 * e00 + w01 * e01)
    g = g - (w00 * e10 + w01 * e11)
    h = h - (w10 * e10 + w11 * e11)
    rest = 1.0 / (f * h - g * g)
    u = r[2] - (w00 * r[0] + w01 * r[1])
    v = r[3] - (w10 * r[0] + w11 * r[1])
    n2, n3 = (h * u - g * v) * rest, (f * v - g * u) * rest
    n0 = (d * r[0] - q * r[1]) * inv - (w00 * n2 + w10 * n3)
    n1 = (a * r[1] - q * r[0]) * inv - (w01 * n2 + w11 * n3)
    new = panel - ((c[0] * n0 + c[1] * n1) + (c[2] * n2 + c[3] * n3))
    for i, row in enumerate((n0, n1, n2, n3)):
        new = jnp.where(at == t + i, row, new)
    return new


def eliminate(grid):
    panels = [grid[8 * i:8 * i + 8] for i in range(8)]
    for b in range(8):
        columns = [
            [lane(panels[i], 8 * b + t) for t in range(8)] if i != b else None
            for i in range(8)
        ]
        done = pivot_four(pivot_four(panels[b], 8 * b, 0), 8 * b, 4)
        rows = [sub(done, t) for t in range(8)]
        for i in range(8):
            if i != b:
                m = [columns[i][t] * rows[t] for t in range(8)]
                panels[i] = panels[i] - (
                    ((m[0] + m[1]) + (m[2] + m[3])) + ((m[4] + m[5]) + (m[6] + m[7]))
                )
        panels[b] = done
    return jnp.concatenate(panels, axis=0)


def apply_kernel(sums_ref, et_hbm, out_ref, full, et_ref, et_sem):
    load = pltpu.make_async_copy(et_hbm, et_ref, et_sem)
    load.start()
    low, high = sums_ref[0], sums_ref[1]
    both = jnp.concatenate(
        [low, pltpu.roll(low, 64, 1), high, pltpu.roll(high, 64, 1)], axis=0
    )
    row_at = lax.broadcasted_iota(jnp.int32, (MEMBERS, 2 * MEMBERS), 0)
    lane_at = lax.broadcasted_iota(jnp.int32, (MEMBERS, 2 * MEMBERS), 1)
    left = lane_at < MEMBERS
    r_col = jnp.sum(jnp.where(left, both, 0.0), axis=1, keepdims=True) * (1.0 / MEMBERS)
    eye = jnp.where(row_at == lane_at, 1.0, 0.0)
    grid = eliminate(
        jnp.where(
            left, (both - r_col) + eye, jnp.where(lane_at - MEMBERS == row_at, 1.0, 0.0)
        )
    )
    inverse = jnp.where(left, pltpu.roll(grid, 64, 1), 0.0)
    shift = jnp.sum(inverse * r_col, axis=0, keepdims=True)
    gain_t = jnp.where(left, shift - ROOT * (eye - inverse), 0.0)
    centre = jnp.sum(gain_t, axis=1, keepdims=True) * (1.0 / MEMBERS)
    moves = jnp.where(left, (gain_t - centre) * (1.0 / ROOT), 0.0)
    one = moves.astype(BF16).astype(F32)
    two = (moves - one).astype(BF16).astype(F32)
    three = moves - one - two
    factors = jnp.concatenate(
        [(one + pltpu.roll(two, 64, 1)).astype(BF16), three.astype(BF16)], axis=1
    )
    zero = jnp.zeros((MEMBERS, 2 * BLOCK), BF16)
    load.wait()
    for g in range(LROWS // 2):
        at = 2 * g * MEMBERS
        pair = jnp.concatenate(
            [et_ref[at:at + MEMBERS, :], et_ref[at + MEMBERS:at + 2 * MEMBERS, :]], axis=1
        )
        moved = pair.astype(F32) + jnp.dot(
            factors, jnp.concatenate([pair, pair, pair, zero], axis=0),
            preferred_element_type=F32,
        )
        full[pl.ds(2 * g, MEMBERS, stride=LROWS), :] = moved[:, 0:BLOCK]
        full[pl.ds(2 * g + 1, MEMBERS, stride=LROWS), :] = moved[:, BLOCK:2 * BLOCK]
    out_ref[...] = full[...].astype(BF16)


def on_device(ensemble, row_profile, col_profile, obs_owned, noise_owned, block_owner):
    hbm = pl.BlockSpec(memory_space=pltpu.HBM)
    vmem = pl.BlockSpec(memory_space=pltpu.VMEM)
    dma = pltpu.SemaphoreType.DMA
    size = MEMBERS * LROWS
    sums, field_t = pl.pallas_call(
        partial_kernel,
        name="partial_sums",
        out_shape=(
            jax.ShapeDtypeStruct((2, 16, BLOCK), F32),
            jax.ShapeDtypeStruct((size, LCOLS), BF16),
        ),
        in_specs=[hbm] * 6,
        out_specs=(vmem, hbm),
        scratch_shapes=[
            pltpu.VMEM((3, MEMBERS, 16, LCOLS), BF16),
            pltpu.VMEM((3, size // 3, LCOLS), F32),
            pltpu.VMEM((size, LCOLS), F32),
            pltpu.VMEM((size, LCOLS), F32),
            pltpu.VMEM((size, 2 * LCOLS), BF16),
            pltpu.VMEM((2, STEPS, LCOLS, WIDE), BF16),
            pltpu.VMEM((STEPS, LROWS, WIDE), BF16),
            pltpu.VMEM((STEPS, LCOLS, WIDE), F32),
            pltpu.VMEM((STEPS, LCOLS, WIDE), F32),
            pltpu.VMEM((2 * LCOLS, WIDE), BF16),
            pltpu.VMEM((LROWS, WIDE), F32),
            pltpu.VMEM((STEPS, 4, 24, BLOCK), F32),
            pltpu.VMEM((STEPS, 4, 16, BLOCK), F32),
            pltpu.VMEM((STEPS, 4, 24, BLOCK), F32),
            pltpu.VMEM((3, 4, 4, 24, BLOCK), F32),
            pltpu.VMEM((3, 4, 24, BLOCK), F32),
            pltpu.VMEM((3, 24, BLOCK), F32),
            pltpu.VMEM((4, 3, 4, 16, BLOCK), F32),
            pltpu.VMEM((4, 3, 16, BLOCK), F32),
            pltpu.VMEM((3, 16, BLOCK), F32),
            pltpu.VMEM((STEPS, 3, 24, BLOCK), F32),
            pltpu.VMEM((3, 4, 24, BLOCK), F32),
            pltpu.VMEM((3, 24, BLOCK), F32),
            pltpu.VMEM((128, 8, BLOCK), F32),
            pltpu.VMEM((8, BLOCK), F32),
            pltpu.VMEM((20, 16, BLOCK), F32),
            pltpu.VMEM((5, 2, 16, BLOCK), F32),
            pltpu.VMEM((1, CAP * BLOCK), F32),
            pltpu.VMEM((1, CAP * BLOCK), F32),
            pltpu.SMEM((1, BLOCK), jnp.int32),
            pltpu.VMEM((1, BLOCK), jnp.int32),
            dma((4,)),
            dma((3,)), dma, dma((2, STEPS)), dma((STEPS,)),
            dma, dma((3,)), dma, dma((STEPS,)),
            dma((3,)), dma((3,)), dma((3,)),
            dma((3, 4)), dma((3,)), dma((3,)),
            dma((4, 3)), dma((4, 3)), dma((3,)),
            dma((STEPS, 3)), dma((3, 4)), dma((3,)),
            dma, dma((3,)), dma((3,)), dma((3,)), dma,
            dma((20,)), dma((20,)),
        ],
        compiler_params=pltpu.CompilerParams(
            collective_id=0, has_side_effects=True, vmem_limit_bytes=62 << 20
        ),
    )(ensemble, col_profile, row_profile, obs_owned, noise_owned, block_owner.reshape(1, -1))
    moved = pl.pallas_call(
        apply_kernel,
        name="solve_apply",
        out_shape=jax.ShapeDtypeStruct((size, LCOLS), BF16),
        in_specs=[vmem, hbm],
        out_specs=vmem,
        scratch_shapes=[
            pltpu.VMEM((size, LCOLS), F32), pltpu.VMEM((size, LCOLS), BF16), dma
        ],
        compiler_params=pltpu.CompilerParams(vmem_limit_bytes=62 << 20),
    )(sums, field_t)
    return moved.reshape(ensemble.shape)


def solution(mesh):
    in_specs = (
        P(None, "rows", "cols"),
        P("rows", None),
        P("cols", None),
        P(("rows", "cols"), None),
        P(("rows", "cols"), None),
        P(),
    )
    return jax.shard_map(
        on_device, mesh=mesh, in_specs=in_specs, out_specs=P(None, "rows", "cols"),
        check_vma=False,
    )
```

```python
import functools
import math

import jax
import jax.numpy as jnp
from jax import lax
from jax.experimental import pallas as pl
from jax.experimental.pallas import tpu as pltpu
from jax.sharding import PartitionSpec as P

MEMBERS = 64
BLOCK = 128
CAP = 3
LROWS = 48
LCOLS = 128
STEPS = 16
WIDE = 512
AHEAD = 3
LAG2 = 3
LAG3 = 6
ROOT = math.sqrt(MEMBERS - 1)
MESH = pl.DeviceIdType.MESH
F32 = jnp.float32
BF16 = jnp.bfloat16


def here():
    r = lax.axis_index("rows")
    c = lax.axis_index("cols")
    return r // 4, r % 4, c // 2, c % 2


def device(y, x, z, k):
    return (y * 4 + x, z * 2 + k)


def partial_kernel(
    e_hbm, col_hbm, row_hbm, obs_hbm, noise_hbm, owner_hbm,
    sums_ref, et_hbm,
    e_v, ef, esend, erecv, lhs, col_v, row_v, csend, crecv, rhs, rowf, pa, pb, pc,
    ra1, ra2, ra3, rb1, rb2, rb3, rc1, rc2, rc3, slots, pack, got_core, got,
    obs_ref, noise_ref, owner_ref, owner_row, small_sem,
    e_sem, et_sem, col_sem, row_sem,
    es_sem, er_sem, cs_sem, cr_sem,
    sa, sb, sc,
    qa1, qa2, qa3, qb1, qb2, qb3, qc1, qc2, qc3,
    so, qo_z, qo_x, qo_y, qo_k,
    st, qt,
):
    y, x, z, k = here()
    sibling = device(y, x, z, 1 - k)
    turn = 1 - 2 * k

    def zpeer(d):
        return device(y, x, (z + turn * d + 4) % 4, k)

    def xpeer(d):
        return device(y, (x + turn * d + 4) % 4, z, k)

    def ypeer(d):
        return device((y + turn * d + 4) % 4, x, z, k)

    def flat(d):
        return device((y + d // 4) % 4, (x + d % 4) % 4, z, k)

    def remote(src, dst, send, recv, to):
        return pltpu.make_async_remote_copy(
            src_ref=src, dst_ref=dst, send_sem=send, recv_sem=recv,
            device_id=to, device_id_type=MESH,
        )

    def sent(src, sem):
        remote(src, src, sem, sem, sibling).wait_send()

    def landed(dst, sem):
        remote(dst, dst, sem, sem, sibling).wait_recv()

    def span(core, s):
        dz, dx = 3 - s // 4, 3 - s % 4
        way = 1 - 2 * core
        to_z, to_x = (z + way * dz + 4) % 4, (x + way * dx + 4) % 4
        first = ((core * 4 + to_z) * 4 + to_x) * WIDE
        return pl.ds(pl.multiple_of(first, WIDE), WIDE)

    def load_col(which, s):
        core = k if which == 0 else 1 - k
        return pltpu.make_async_copy(
            col_hbm.at[:, span(core, s)], col_v.at[which, s], col_sem.at[which, s]
        )

    def load_row(s):
        return pltpu.make_async_copy(
            row_hbm.at[:, span(k, s)], row_v.at[s], row_sem.at[s]
        )

    load_e = [
        pltpu.make_async_copy(
            e_hbm.at[:, pl.ds(16 * i, 16), :], e_v.at[i], e_sem.at[i]
        )
        for i in range(3)
    ]
    for load in load_e:
        load.start()
    load_small = [
        pltpu.make_async_copy(src, dst, small_sem.at[i])
        for i, (src, dst) in enumerate(
            ((obs_hbm, obs_ref), (noise_hbm, noise_ref), (owner_hbm, owner_ref),
             (owner_hbm, owner_row))
        )
    ]
    for load in load_small:
        load.start()

    barrier = pltpu.get_barrier_semaphore()
    pl.semaphore_signal(barrier, 1, device_id=sibling, device_id_type=MESH)
    for peer in [
        flat(d) for d in (10, 9, 11, 6, 14, 5, 7, 13, 15, 8, 2, 4, 12, 1, 3)
    ] + [zpeer(d) for d in (2, 1, 3)]:
        pl.semaphore_signal(barrier, 1, device_id=peer, device_id_type=MESH)

    def start_loads(s, carry):
        load_col(1, s).start()
        load_col(0, s).start()
        load_row(s).start()
        return carry

    lax.fori_loop(0, STEPS, start_loads, 0)

    home = k * 64 + (x * 4 + y) * 4 + z
    pack[...] = jnp.zeros_like(pack)
    for load in load_small:
        load.wait()
    for i in range(CAP):
        pack[i:i + 1, :] = obs_ref[:, i * BLOCK:(i + 1) * BLOCK]
        pack[4 + i:5 + i, :] = noise_ref[:, i * BLOCK:(i + 1) * BLOCK]
    slots[home] = pack[...]

    pl.semaphore_wait(barrier, 19)

    for d in (1, 2, 3):
        remote(slots.at[home], slots.at[home], so, qo_z.at[d - 1], zpeer(d)).start()

    third = MEMBERS * LROWS // 3
    for piece in range(3):
        load_e[piece].wait()
        ef[piece] = e_v[piece].astype(F32).reshape(third, LCOLS)
        for i in range(16):
            at = piece * 16 + i
            plane = ef[piece, pl.ds(i, MEMBERS, stride=16), :]
            esend[at * MEMBERS:(at + 1) * MEMBERS, :] = plane
            lhs[at * MEMBERS:(at + 1) * MEMBERS, 0:LCOLS] = plane.astype(BF16)
        rows = pl.ds(piece * third, third)
        remote(
            esend.at[rows], erecv.at[rows], es_sem, er_sem.at[piece], sibling
        ).start()

    def send_col(s):
        load_col(1, s).wait()
        csend[s] = col_v[1, s].astype(F32)
        remote(csend.at[s], crecv.at[s], cs_sem, cr_sem.at[s], sibling).start()

    for s in range(AHEAD):
        send_col(s)

    for piece in range(3):
        landed(erecv.at[pl.ds(piece * third, third)], er_sem.at[piece])
        lhs[piece * third:(piece + 1) * third, LCOLS:2 * LCOLS] = (
            erecv[piece * third:(piece + 1) * third, :].astype(BF16)
        )
    save_et = pltpu.make_async_copy(lhs.at[:, pl.ds(0, LCOLS)], et_hbm, et_sem)
    save_et.start()

    def compute(s):
        load_col(0, s).wait()
        load_row(s).wait()
        landed(crecv.at[s], cr_sem.at[s])
        rhs[0:LCOLS, :] = col_v[0, s]
        rhs[LCOLS:2 * LCOLS, :] = crecv[s].astype(BF16)
        rowf[...] = row_v[s].astype(F32)
        total = jnp.zeros((MEMBERS, WIDE), F32)
        group = 4
        for g in range(LROWS // group):
            rows = group * MEMBERS
            along = jnp.dot(
                lhs[g * rows:(g + 1) * rows, :], rhs[...], preferred_element_type=F32
            )
            for i in range(group):
                at = g * group + i
                total += along[i * MEMBERS:(i + 1) * MEMBERS] * rowf[at:at + 1, :]
        for q in range(4):
            lanes = slice(q * BLOCK, (q + 1) * BLOCK)
            place = (turn * (q - y) + 4) % 4
            pa[s, place] = total[0:24, lanes]
            pb[s, place] = total[24:40, lanes]
            pc[s, place] = total[40:64, lanes]

    def first_sends(w, j):
        s, dz, dx = 4 * w + j, 3 - w, 3 - j

        @pl.when(dz != 0)
        def _():
            remote(
                pa.at[s], ra1.at[dz - 1, j],
                sa.at[0], qa1.at[dz - 1, j], zpeer(dz),
            ).start()

        if dx != 0:
            remote(
                pb.at[s], rb1.at[w, dx - 1],
                sb.at[0], qb1.at[w, dx - 1], xpeer(dx),
            ).start()

        for d in (2, 1, 3):
            remote(
                pc.at[s, d], rc1.at[s, d - 1],
                sc.at[0], qc1.at[s, d - 1], ypeer(d),
            ).start()

    def second_a(w, j):
        s, dz, dx = 4 * w + j, 3 - w, 3 - j

        @pl.when(dz == 0)
        def _():
            for p in range(3):
                landed(ra1.at[p, j], qa1.at[p, j])
            pa[s] = pa[s] + (
                ra1[0, j] + (ra1[1, j] + ra1[2, j])
            )

            if dx != 0:
                remote(
                    pa.at[s], ra2.at[dx - 1],
                    sa.at[1], qa2.at[dx - 1], xpeer(dx),
                ).start()

    def second_b(w, j):
        s, dz, dx = 4 * w + j, 3 - w, 3 - j

        if dx == 0:
            for p in range(3):
                landed(rb1.at[w, p], qb1.at[w, p])
            pb[s] = pb[s] + (rb1[w, 0] + (rb1[w, 1] + rb1[w, 2]))
            for d in (2, 1, 3):
                remote(
                    pb.at[s, d], rb2.at[w, d - 1],
                    sb.at[1], qb2.at[w, d - 1], ypeer(d),
                ).start()

    def second_c(w, j):
        s, dz, dx = 4 * w + j, 3 - w, 3 - j
        for p in range(3):
            landed(rc1.at[s, p], qc1.at[s, p])
        pc[s, 0] = pc[s, 0] + (rc1[s, 0] + (rc1[s, 1] + rc1[s, 2]))

        @pl.when(dz != 0)
        def _():
            remote(
                pc.at[s, 0], rc2.at[dz - 1, j],
                sc.at[1], qc2.at[dz - 1, j], zpeer(dz),
            ).start()

    def third_a():
        s = STEPS - 1
        for p in range(3):
            landed(ra2.at[p], qa2.at[p])
        pa[s] = pa[s] + (ra2[0] + (ra2[1] + ra2[2]))
        for d in (2, 1, 3):
            remote(
                pa.at[s, d], ra3.at[d - 1],
                sa.at[2], qa3.at[d - 1], ypeer(d),
            ).start()

    def third_b(w, j):
        s, dz, dx = 4 * w + j, 3 - w, 3 - j

        if dx == 0:
            for p in range(3):
                landed(rb2.at[w, p], qb2.at[w, p])
            pb[s, 0] = pb[s, 0] + (rb2[w, 0] + (rb2[w, 1] + rb2[w, 2]))

            @pl.when(dz != 0)
            def _():
                remote(
                    pb.at[s, 0], rb3.at[dz - 1],
                    sb.at[2], qb3.at[dz - 1], zpeer(dz),
                ).start()

    def third_c(w, j):
        s, dz, dx = 4 * w + j, 3 - w, 3 - j

        @pl.when(dz == 0)
        def _():
            for p in range(3):
                landed(rc2.at[p, j], qc2.at[p, j])
            pc[s, 0] = pc[s, 0] + (
                rc2[0, j] + (rc2[1, j] + rc2[2, j])
            )

            if dx != 0:
                remote(
                    pc.at[s, 0], rc3.at[dx - 1],
                    sc.at[2], qc3.at[dx - 1], xpeer(dx),
                ).start()

    base_y = k * 64 + (x * 4 + y) * 4
    base_x = k * 64 + x * 16
    base_k = k * 64

    def slots_y():
        for d in (1, 2, 3):
            landed(slots.at[home], qo_z.at[d - 1])
        mine = slots.at[pl.ds(base_y, 4)]
        for d in (1, 2, 3):
            remote(mine, mine, so, qo_y.at[d - 1], ypeer(d)).start()

    def slots_x():
        for d in (1, 2, 3):
            landed(slots.at[pl.ds(base_y, 4)], qo_y.at[d - 1])
        mine = slots.at[pl.ds(base_x, 16)]
        for d in (1, 2, 3):
            remote(mine, mine, so, qo_x.at[d - 1], xpeer(d)).start()

    def slots_k():
        for d in (1, 2, 3):
            landed(slots.at[pl.ds(base_x, 16)], qo_x.at[d - 1])
        mine = slots.at[pl.ds(base_k, 64)]
        remote(mine, mine, so, qo_k, sibling).start()

    def lagged(events, w, j, lag):
        back = (j - lag) // 4
        late, at = w + back, (j - lag) % 4

        def run():
            for event in events:
                event(late, at)

        if back == 0:
            run()
        else:
            pl.when(late >= 0)(run)

    def phase(w, carry):
        for j in range(4):
            s = 4 * w + j
            pl.when(s + AHEAD < STEPS)(functools.partial(send_col, s + AHEAD))
            compute(s)
            first_sends(w, j)
            second_a(w, j)
            lagged((second_b,), w, j, 2)
            lagged((second_c, third_c), w, j, 3)
            lagged((third_b,), w, j, 5)
        pl.when(w == 0)(slots_x)
        pl.when(w == 1)(slots_k)
        return carry

    slots_y()
    lax.fori_loop(0, STEPS // 4, phase, 0)

    last = STEPS - 1
    second_c(3, 1)
    third_c(3, 1)
    third_b(2, 3)
    second_b(3, 3)
    third_a()
    second_c(3, 2)
    third_c(3, 2)
    second_c(3, 3)
    third_c(3, 3)
    third_b(3, 3)

    landed(slots.at[pl.ds(base_k, 64)], qo_k)
    me = ((k * 4 + z) * 4 + x) * 4 + y
    owner = owner_ref[0, me]
    owners = owner_row[...]
    block_at = lax.broadcasted_iota(jnp.int32, (1, BLOCK), 1)
    before = jnp.logical_and(owners == owner, block_at < me)
    rank = jnp.sum(jnp.where(before, 1.0, 0.0), axis=1, keepdims=True)
    o_row, o_col = owner // 8, owner % 8
    found = slots[
        (o_col % 2) * 64 + (o_row % 4) * 16 + (o_row // 4) * 4 + o_col // 2
    ]
    observed = jnp.where(
        rank < 0.5, found[0:1], jnp.where(rank < 1.5, found[1:2], found[2:3])
    )
    variance = jnp.where(
        rank < 0.5, found[4:5], jnp.where(rank < 1.5, found[5:6], found[6:7])
    )
    weight = 1.0 / variance

    for d in range(3):
        landed(ra3.at[d], qa3.at[d])
        landed(rb3.at[d], qb3.at[d])
        landed(rc3.at[d], qc3.at[d])
    predictions = jnp.concatenate(
        [
            pa[last, 0] + (ra3[0] + (ra3[1] + ra3[2])),
            pb[last, 0] + (rb3[0] + (rb3[1] + rb3[2])),
            pc[last, 0] + (rc3[0] + (rc3[1] + rc3[2])),
        ],
        axis=0,
    )
    mean = jnp.mean(predictions, axis=0, keepdims=True)
    anomalies = (predictions - mean) * (1.0 / ROOT)
    scaled = anomalies * weight
    target = anomalies + (observed - mean)
    blank = jnp.zeros((MEMBERS, BLOCK), F32)
    contract = (((1,), (1,)), ((), ()))
    left = jnp.concatenate([scaled[0:16], scaled[32:48]], axis=0)
    right = jnp.concatenate([scaled[16:32], scaled[48:64]], axis=0)
    packed = lax.dot_general(
        left, jnp.concatenate([target, blank], axis=0), contract,
        precision=lax.Precision.HIGHEST, preferred_element_type=F32,
    ) + lax.dot_general(
        right, jnp.concatenate([blank, target], axis=0), contract,
        precision=lax.Precision.HIGHEST, preferred_element_type=F32,
    )
    got[0, 0] = packed[0:16]
    got[0, 1] = packed[16:32]

    remote(got.at[0, 1 - k], got_core.at[0], st.at[0], qt.at[0], sibling).start()
    landed(got_core.at[0], qt.at[0])
    got[1, 0] = got[0, k] + got_core[0]
    for d in (2, 1, 3):
        remote(
            got.at[1, 0], got_core.at[d], st.at[d], qt.at[d], zpeer(d)
        ).start()
    for d in (1, 2, 3):
        landed(got_core.at[d], qt.at[d])
    got[2, 0] = got[1, 0] + (got_core[1] + (got_core[2] + got_core[3]))
    for d in (10, 9, 11, 6, 14, 5, 7, 13, 15, 8, 2, 4, 12, 1, 3):
        remote(
            got.at[2, 0], got_core.at[3 + d], st.at[3 + d], qt.at[3 + d], flat(d)
        ).start()
    total = got[2, 0]
    for d in range(1, 16):
        landed(got_core.at[3 + d], qt.at[3 + d])
        total += got_core[3 + d]
    got[3, 0] = total
    end = 19
    whole = 3
    remote(got.at[whole, 0], got_core.at[end], st.at[end], qt.at[end], sibling).start()
    sums_ref[k] = got[whole, 0]
    landed(got_core.at[end], qt.at[end])
    sums_ref[1 - k] = got_core[end]

    save_et.wait()
    sent(esend, es_sem)
    sent(csend, cs_sem)
    sent(pa.at[pl.ds(0, 12), :], sa.at[0])
    sent(pa.at[pl.ds(0, 3), :], sa.at[1])
    sent(pa.at[0, pl.ds(0, 3)], sa.at[2])
    sent(pb.at[pl.ds(0, 12), :], sb.at[0])
    sent(pb.at[pl.ds(0, 4), pl.ds(0, 3)], sb.at[1])
    sent(pb.at[0, pl.ds(0, 3)], sb.at[2])
    sent(pc.at[pl.ds(0, 16), pl.ds(0, 3)], sc.at[0])
    sent(pc.at[pl.ds(0, 12), 0], sc.at[1])
    sent(pc.at[0, pl.ds(0, 3)], sc.at[2])
    sent(slots.at[pl.ds(0, 3 + 12 + 48 + 64)], so)
    for i in range(20):
        sent(got_core.at[0], st.at[i])


def lane(panel, at):
    return jnp.broadcast_to(panel[:, at:at + 1], panel.shape)


def sub(panel, at):
    return jnp.broadcast_to(panel[at:at + 1], panel.shape)


def pivot_four(panel, column, t):
    at = lax.broadcasted_iota(jnp.int32, panel.shape, 0)
    c = [lane(panel, column + t + i) for i in range(4)]
    r = [sub(panel, t + i) for i in range(4)]
    a, q, d = sub(c[0], t), sub(c[0], t + 1), sub(c[1], t + 1)
    e00, e01, e10, e11 = (
        sub(c[0], t + 2), sub(c[1], t + 2), sub(c[0], t + 3), sub(c[1], t + 3)
    )
    f, g, h = sub(c[2], t + 2), sub(c[2], t + 3), sub(c[3], t + 3)
    inv = 1.0 / (a * d - q * q)
    w00, w01 = (e00 * d - e01 * q) * inv, (e01 * a - e00 * q) * inv
    w10, w11 = (e10 * d - e11 * q) * inv, (e11 * a - e10 * q) * inv
    f = f - (w00 * e00 + w01 * e01)
    g = g - (w00 * e10 + w01 * e11)
    h = h - (w10 * e10 + w11 * e11)
    rest = 1.0 / (f * h - g * g)
    u = r[2] - (w00 * r[0] + w01 * r[1])
    v = r[3] - (w10 * r[0] + w11 * r[1])
    n2, n3 = (h * u - g * v) * rest, (f * v - g * u) * rest
    n0 = (d * r[0] - q * r[1]) * inv - (w00 * n2 + w10 * n3)
    n1 = (a * r[1] - q * r[0]) * inv - (w01 * n2 + w11 * n3)
    new = panel - ((c[0] * n0 + c[1] * n1) + (c[2] * n2 + c[3] * n3))
    for i, row in enumerate((n0, n1, n2, n3)):
        new = jnp.where(at == t + i, row, new)
    return new


def eliminate(grid):
    panels = [grid[8 * i:8 * i + 8] for i in range(8)]
    for b in range(8):
        columns = [
            [lane(panels[i], 8 * b + t) for t in range(8)] if i != b else None
            for i in range(8)
        ]
        done = pivot_four(pivot_four(panels[b], 8 * b, 0), 8 * b, 4)
        rows = [sub(done, t) for t in range(8)]
        for i in range(8):
            if i != b:
                m = [columns[i][t] * rows[t] for t in range(8)]
                panels[i] = panels[i] - (
                    ((m[0] + m[1]) + (m[2] + m[3])) + ((m[4] + m[5]) + (m[6] + m[7]))
                )
        panels[b] = done
    return jnp.concatenate(panels, axis=0)


def apply_kernel(sums_ref, et_hbm, out_ref, full, et_ref, et_sem):
    load = pltpu.make_async_copy(et_hbm, et_ref, et_sem)
    load.start()
    low, high = sums_ref[0], sums_ref[1]
    both = jnp.concatenate(
        [low, pltpu.roll(low, 64, 1), high, pltpu.roll(high, 64, 1)], axis=0
    )
    row_at = lax.broadcasted_iota(jnp.int32, (MEMBERS, 2 * MEMBERS), 0)
    lane_at = lax.broadcasted_iota(jnp.int32, (MEMBERS, 2 * MEMBERS), 1)
    left = lane_at < MEMBERS
    r_col = jnp.sum(jnp.where(left, both, 0.0), axis=1, keepdims=True) * (1.0 / MEMBERS)
    eye = jnp.where(row_at == lane_at, 1.0, 0.0)
    grid = eliminate(
        jnp.where(
            left, (both - r_col) + eye, jnp.where(lane_at - MEMBERS == row_at, 1.0, 0.0)
        )
    )
    inverse = jnp.where(left, pltpu.roll(grid, 64, 1), 0.0)
    shift = jnp.sum(inverse * r_col, axis=0, keepdims=True)
    gain_t = jnp.where(left, shift - ROOT * (eye - inverse), 0.0)
    centre = jnp.sum(gain_t, axis=1, keepdims=True) * (1.0 / MEMBERS)
    moves = jnp.where(left, (gain_t - centre) * (1.0 / ROOT), 0.0)
    one = moves.astype(BF16).astype(F32)
    two = (moves - one).astype(BF16).astype(F32)
    three = moves - one - two
    factors = jnp.concatenate(
        [(one + pltpu.roll(two, 64, 1)).astype(BF16), three.astype(BF16)], axis=1
    )
    zero = jnp.zeros((MEMBERS, 2 * BLOCK), BF16)
    load.wait()
    for g in range(LROWS // 2):
        at = 2 * g * MEMBERS
        pair = jnp.concatenate(
            [et_ref[at:at + MEMBERS, :], et_ref[at + MEMBERS:at + 2 * MEMBERS, :]], axis=1
        )
        moved = pair.astype(F32) + jnp.dot(
            factors, jnp.concatenate([pair, pair, pair, zero], axis=0),
            preferred_element_type=F32,
        )
        full[pl.ds(2 * g, MEMBERS, stride=LROWS), :] = moved[:, 0:BLOCK]
        full[pl.ds(2 * g + 1, MEMBERS, stride=LROWS), :] = moved[:, BLOCK:2 * BLOCK]
    out_ref[...] = full[...].astype(BF16)


def on_device(ensemble, row_profile, col_profile, obs_owned, noise_owned, block_owner):
    hbm = pl.BlockSpec(memory_space=pltpu.HBM)
    vmem = pl.BlockSpec(memory_space=pltpu.VMEM)
    dma = pltpu.SemaphoreType.DMA
    size = MEMBERS * LROWS
    sums, field_t = pl.pallas_call(
        partial_kernel,
        name="partial_sums",
        out_shape=(
            jax.ShapeDtypeStruct((2, 16, BLOCK), F32),
            jax.ShapeDtypeStruct((size, LCOLS), BF16),
        ),
        in_specs=[hbm] * 6,
        out_specs=(vmem, hbm),
        scratch_shapes=[
            pltpu.VMEM((3, MEMBERS, 16, LCOLS), BF16),
            pltpu.VMEM((3, size // 3, LCOLS), F32),
            pltpu.VMEM((size, LCOLS), F32),
            pltpu.VMEM((size, LCOLS), F32),
            pltpu.VMEM((size, 2 * LCOLS), BF16),
            pltpu.VMEM((2, STEPS, LCOLS, WIDE), BF16),
            pltpu.VMEM((STEPS, LROWS, WIDE), BF16),
            pltpu.VMEM((STEPS, LCOLS, WIDE), F32),
            pltpu.VMEM((STEPS, LCOLS, WIDE), F32),
            pltpu.VMEM((2 * LCOLS, WIDE), BF16),
            pltpu.VMEM((LROWS, WIDE), F32),
            pltpu.VMEM((STEPS, 4, 24, BLOCK), F32),
            pltpu.VMEM((STEPS, 4, 16, BLOCK), F32),
            pltpu.VMEM((STEPS, 4, 24, BLOCK), F32),
            pltpu.VMEM((3, 4, 4, 24, BLOCK), F32),
            pltpu.VMEM((3, 4, 24, BLOCK), F32),
            pltpu.VMEM((3, 24, BLOCK), F32),
            pltpu.VMEM((4, 3, 4, 16, BLOCK), F32),
            pltpu.VMEM((4, 3, 16, BLOCK), F32),
            pltpu.VMEM((3, 16, BLOCK), F32),
            pltpu.VMEM((STEPS, 3, 24, BLOCK), F32),
            pltpu.VMEM((3, 4, 24, BLOCK), F32),
            pltpu.VMEM((3, 24, BLOCK), F32),
            pltpu.VMEM((128, 8, BLOCK), F32),
            pltpu.VMEM((8, BLOCK), F32),
            pltpu.VMEM((20, 16, BLOCK), F32),
            pltpu.VMEM((5, 2, 16, BLOCK), F32),
            pltpu.VMEM((1, CAP * BLOCK), F32),
            pltpu.VMEM((1, CAP * BLOCK), F32),
            pltpu.SMEM((1, BLOCK), jnp.int32),
            pltpu.VMEM((1, BLOCK), jnp.int32),
            dma((4,)),
            dma((3,)), dma, dma((2, STEPS)), dma((STEPS,)),
            dma, dma((3,)), dma, dma((STEPS,)),
            dma((3,)), dma((3,)), dma((3,)),
            dma((3, 4)), dma((3,)), dma((3,)),
            dma((4, 3)), dma((4, 3)), dma((3,)),
            dma((STEPS, 3)), dma((3, 4)), dma((3,)),
            dma, dma((3,)), dma((3,)), dma((3,)), dma,
            dma((20,)), dma((20,)),
        ],
        compiler_params=pltpu.CompilerParams(
            collective_id=0, has_side_effects=True, vmem_limit_bytes=62 << 20
        ),
    )(ensemble, col_profile, row_profile, obs_owned, noise_owned, block_owner.reshape(1, -1))
    moved = pl.pallas_call(
        apply_kernel,
        name="solve_apply",
        out_shape=jax.ShapeDtypeStruct((size, LCOLS), BF16),
        in_specs=[vmem, hbm],
        out_specs=vmem,
        scratch_shapes=[
            pltpu.VMEM((size, LCOLS), F32), pltpu.VMEM((size, LCOLS), BF16), dma
        ],
        compiler_params=pltpu.CompilerParams(vmem_limit_bytes=62 << 20),
    )(sums, field_t)
    return moved.reshape(ensemble.shape)


def solution(mesh):
    in_specs = (
        P(None, "rows", "cols"),
        P("rows", None),
        P("cols", None),
        P(("rows", "cols"), None),
        P(("rows", "cols"), None),
        P(),
    )
    return jax.shard_map(
        on_device, mesh=mesh, in_specs=in_specs, out_specs=P(None, "rows", "cols"),
        check_vma=False,
    )
```
